32 devices in a mesh: gx: 8 (over y, x, core), gy: 4 (over z).
Axes of the slice: x: 2, y: 2, z: 4, core: 2. Of those that a mesh axis runs over, the one named last changes fastest.
Arguments:
- object_field: float32 [2, 8192, 4096], P(None, 'gx', 'gy'), may hold values from -5 to 5
- probe: float32 [2, 256, 256], replicated, may hold values from -5 to 5
- centers: int32 [512, 2], P(('gx', 'gy')), may hold values from 0 to 1023
- live: int32 [512], P(('gx', 'gy')), may hold values from 0 to 1, as said below
- measured: float32 [512, 256, 256], P(('gx', 'gy')), may hold values from 0.5 to 2.5
Outputs:
- object_grad: float32 [2, 8192, 4096], P(None, 'gx', 'gy')
- probe_grad: float32 [2, 256, 256], replicated
- slot_loss: float32 [512], P(('gx', 'gy'))
The draws below stay inside these ranges and needn't reach their ends.
Inputs may be any that keep to these rules, and one draw needn't show every extreme that they name: In each tile's 16 slots the live ones come first; every tile has at least one live slot, and some tile has all 16 live.
All inputs are finite; a program needn't handle non-finite values.
Results may differ from the reference program's by a relative error of at most 0.0001.
Values sent between devices are 32-bit elements; how exact they have to be, the bound alone decides.
No kernel may reach another device: no remote copies, remote signals or barrier semaphores. Data moves between devices by JAX's collectives and lax.ppermute only.
A program may use at most 192 MiB of HBM per device.

```python
import math
import jax
import jax.numpy as jnp
from jax import lax

M = 256
HALF = 128
TILE = 1024
PSLOT = 16
TILES = 32
SLOTS = 512
NR = 8192
NC = 4096
N_GY = 4


def draw_live(key, part):
    counts = jax.random.randint(jax.random.fold_in(key, 11), (TILES,), 1, PSLOT + 1)
    fullest = jax.random.randint(jax.random.fold_in(key, 12), (), 0, TILES)
    counts = jnp.where(jnp.arange(TILES) == fullest, PSLOT, counts)
    slot_pos = jnp.arange(PSLOT)
    return (slot_pos[None, :] < counts[:, None]).astype(jnp.int32).reshape(SLOTS)


def set_ends(entries, own_key, least, largest):
    spot = [jax.random.randint(jax.random.fold_in(own_key, axis), (), 0, length) for axis, length in enumerate(entries.shape)]
    widest = entries.shape.index(max(entries.shape))
    next_to = spot[:widest] + [(spot[widest] + 1) % entries.shape[widest]] + spot[widest + 1:]
    return entries.at[tuple(spot)].set(least).at[tuple(next_to)].set(largest)


def steps_of(key, dims, cuts, low, largest):
    def one(position, blocks):
        heights = jax.random.uniform(jax.random.fold_in(jax.random.fold_in(key, 6), position), (blocks,), jnp.float32, low / len(cuts), largest / len(cuts))
        return jnp.repeat(jnp.exp(heights), dims[position] // blocks).reshape((-1,) + (1,) * (len(dims) - position - 1))

    level = one(*cuts[0])
    for cut in cuts[1:]:
        level = level * one(*cut)
    return level


def bell_draw(stream_key, extent, deviation, most, cuts=(), kind=jnp.bfloat16):
    result = jax.random.normal(stream_key, extent, jnp.float32) * deviation
    if len(cuts) > 0:
        result = steps_of(stream_key, extent, cuts, -0.22, 0.18) * result
    return jnp.clip(result, min=-most, max=most).astype(kind)


def setup_inputs(seed: int = 0) -> dict:
    key_of = jax.random.split(jax.random.key(seed), 6)
    object_field = bell_draw(key_of[0], (2, NR, NC), 0.7, 5.0, ((1, 8), (2, 4)), jnp.float32)
    probe = bell_draw(key_of[1], (2, M, M), 1.0, 5.0, (), jnp.float32)
    centers = set_ends(jax.random.randint(key_of[2], (SLOTS, 2), 0, TILE), jax.random.fold_in(key_of[2], 1), 0, TILE - 1).astype(jnp.int32)
    live = draw_live(jax.random.fold_in(key_of[5], 71), 0)
    measured = jnp.clip(0.5 + 2.0 * jax.random.uniform(key_of[4], (SLOTS, M, M), jnp.float32) ** steps_of(key_of[4], (SLOTS, M, M), ((0, 32),), -0.2, 0.2), 0.5, 2.5)
    return {"object_field": object_field, "probe": probe, "centers": centers, "live": live, "measured": measured}


def reference(object_field, probe, centers, live, measured):
    object_c = lax.complex(object_field[0], object_field[1])
    padded = jnp.pad(object_c, HALF)
    probe_c = lax.complex(probe[0], probe[1])
    slot_ids = jnp.arange(SLOTS, dtype=jnp.int32)
    owners = slot_ids // PSLOT
    row_start = (owners // N_GY * TILE + centers[:, 0]).astype(jnp.int32)
    col_start = (owners % N_GY * TILE + centers[:, 1]).astype(jnp.int32)

    def visit(state_now, slot_index):
        grad_pad, probe_acc = state_now
        row_at = row_start[slot_index]
        col_at = col_start[slot_index]
        patch_obj = lax.dynamic_slice(padded, (row_at, col_at), (M, M))
        farfield = jnp.fft.fft2(probe_c * patch_obj, norm='ortho')
        far_re = jnp.real(farfield)
        far_im = jnp.imag(farfield)
        modulus = jnp.sqrt(far_re * far_re + far_im * far_im + 1.0)
        differ = modulus - measured[slot_index]
        weight = live[slot_index].astype(modulus.dtype)
        adjoint = jnp.fft.ifft2(farfield * (differ / modulus * weight), norm='ortho')
        old_patch = lax.dynamic_slice(grad_pad, (row_at, col_at), (M, M))
        grad_pad = lax.dynamic_update_slice(grad_pad, old_patch + jnp.conj(probe_c) * adjoint, (row_at, col_at))
        probe_acc = probe_acc + jnp.conj(patch_obj) * adjoint
        loss = 0.5 * weight * jnp.sum(differ * differ) / (M * M)
        return ((grad_pad, probe_acc), loss)
    start = (jnp.zeros_like(padded), jnp.zeros_like(probe_c))
    (grad_pad, probe_acc), slot_loss = lax.scan(visit, start, slot_ids)
    inner = grad_pad[HALF:HALF + NR, HALF:HALF + NC]
    object_grad = jnp.stack([jnp.real(inner), jnp.imag(inner)]).astype(jnp.float32)
    probe_grad = (jnp.stack([jnp.real(probe_acc), jnp.imag(probe_acc)]) / math.sqrt(SLOTS)).astype(jnp.float32)
    return (object_grad, probe_grad, slot_loss.astype(jnp.float32))
```

```python
import functools
import math

import jax
import jax.numpy as jnp
import numpy as np
from jax import lax
from jax.experimental import pallas as pl
from jax.experimental.pallas import tpu as pltpu
from jax.sharding import PartitionSpec as P

LANES = 128
SUBS = 8
BF = jnp.bfloat16
F32 = jnp.float32


def split_np(table):
    hi = table.astype(np.float32).astype(jnp.bfloat16)
    lo = (table - hi.astype(np.float64)).astype(np.float32).astype(jnp.bfloat16)
    return hi, lo


def tables_np(extent):
    half = extent // 2
    k = np.arange(extent)[:, None]
    n = np.arange(half)[None, :]
    angle = -2.0 * np.pi * ((k * n) % extent) / extent
    re = np.cos(angle) / math.sqrt(extent)
    im = np.sin(angle) / math.sqrt(extent)
    lefts, rights = [], []
    for parity in range(2):
        a, b = re[parity::2], im[parity::2]
        left = np.block([[a, -b], [b, a]])
        for mat in (left, left.T):
            hi, lo = split_np(mat)
            lefts.append(np.concatenate([hi, lo, hi], axis=1))
            rights.append(np.concatenate([hi, lo, hi], axis=0))
    forward_rows = np.stack([lefts[0], lefts[2]])
    forward_cols = np.stack([rights[1], rights[3]])
    back_cols = np.stack([rights[0], rights[2]])
    back_rows = np.stack([lefts[1], lefts[3]])
    pick = np.zeros((extent, extent), np.float32)
    pick[2 * np.arange(half), np.arange(half)] = 1
    pick[2 * np.arange(half) + 1, half + np.arange(half)] = 1
    pick = np.concatenate([pick, pick], axis=0).astype(jnp.bfloat16)
    return forward_rows, forward_cols, back_cols, back_rows, pick


def parts(x):
    hi = x.astype(BF)
    lo = (x - hi.astype(F32)).astype(BF)
    return hi, lo


def matmul(a, b):
    return jnp.dot(a, b, preferred_element_type=F32)


def slot_kernel(
    phase, extent, slots, tile,
    centers, live, *refs,
):
    half = extent // 2
    inner = phase == "inner"
    it = iter(refs)
    take = lambda n: [next(it) for _ in range(n)]
    tile_hbm, probe, meas_hbm, fr, fc, bc, br, pick = take(8)
    if not inner:
        up_hbm, down_hbm, left_hbm, right_hbm, corner_hbm, grad_in, acc_in, loss_in = take(8)
    grad_out, acc_out, loss_out = take(3)
    if not inner:
        gup, gdown, gleft, gright = take(4)
    ext, grad, shifted, accs, turned, meas, sh_h, sh_l, sems, msems = take(10)
    size = tile + 2 * half
    mid = pl.ds(half, tile)

    loads = []

    def load(src, dst):
        loads.append(pltpu.make_async_copy(src, dst, sems.at[len(loads)]))
        loads[-1].start()

    load(tile_hbm, ext.at[:, mid, mid])
    if not inner:
        load(up_hbm, ext.at[:, pl.ds(0, half), mid])
        load(down_hbm, ext.at[:, pl.ds(half + tile, half), mid])
        load(left_hbm, ext.at[:, mid, pl.ds(0, half)])
        load(right_hbm, ext.at[:, mid, pl.ds(half + tile, half)])
        for i, rows in enumerate((0, half + tile)):
            for j, cols in enumerate((0, half + tile)):
                load(corner_hbm.at[j, i], ext.at[:, pl.ds(rows, half), pl.ds(cols, half)])
        load(grad_in, grad.at[:, mid, mid])
    fetches = [
        pltpu.make_async_copy(meas_hbm.at[:, :, pl.ds(j * LANES, LANES)], meas.at[j], msems.at[j])
        for j in range(2)
    ]
    for f in fetches:
        f.start()

    for p in range(2):
        plane = probe[p]
        for b in range(SUBS):
            shifted[b, p] = pltpu.roll(plane, b, 0) if b else plane
    accs[...] = jnp.zeros_like(accs)
    if inner:
        loss_out[...] = jnp.zeros_like(loss_out)
        zero_rows = jnp.zeros((2, SUBS, size), F32)

        def clear(i, c):
            grad[:, pl.ds(pl.multiple_of(i * SUBS, SUBS), SUBS), :] = zero_rows
            return c

        lax.fori_loop(0, size // SUBS, clear, 0)
    else:
        loss_out[...] = loss_in[...]
        edge = jnp.zeros((2, SUBS, size), F32)

        def clear_rows(i, c):
            at = pl.multiple_of(i * SUBS, SUBS)
            grad[:, pl.ds(at, SUBS), :] = edge
            grad[:, pl.ds(half + tile + at, SUBS), :] = edge
            return c

        lax.fori_loop(0, half // SUBS, clear_rows, 0)
        side = jnp.zeros((2, SUBS, half), F32)

        def clear_cols(i, c):
            at = pl.multiple_of(half + i * SUBS, SUBS)
            grad[:, pl.ds(at, SUBS), pl.ds(0, half)] = side
            grad[:, pl.ds(at, SUBS), pl.ds(half + tile, half)] = side
            return c

        lax.fori_loop(0, tile // SUBS, clear_cols, 0)
    for c in loads:
        c.wait()
    for f in fetches:
        f.wait()

    chunk = 32
    lane8 = lax.broadcasted_iota(jnp.int32, (SUBS, LANES), 1)
    sub8 = lax.broadcasted_iota(jnp.int32, (SUBS, LANES), 0)

    def visit(s):
        row = centers[s, 0]
        col = centers[s, 1]
        b = lax.rem(row, SUBS)
        r = lax.rem(col, LANES)
        a8 = pl.multiple_of(row - b, SUBS)
        q = pl.multiple_of(col - r, LANES)
        lane = lax.broadcasted_iota(jnp.int32, (chunk, LANES), 1)

        def at(off):
            return pl.ds(pl.multiple_of(a8 + off, SUBS), chunk)

        def at8(off):
            return pl.ds(pl.multiple_of(a8 + off, SUBS), SUBS)

        cols = [pl.ds(pl.multiple_of(q + j * LANES, LANES), LANES) for j in range(3)]

        def patch(p, i):
            c0 = jnp.where(lane >= r, ext[p, at(i), cols[0]], ext[p, at(i), cols[2]])
            c1 = ext[p, at(i), cols[1]]
            if i == 0:
                x0 = jnp.where(lane8 >= r, ext[p, at8(extent), cols[0]], ext[p, at8(extent), cols[2]])
                x1 = ext[p, at8(extent), cols[1]]
                c0 = jnp.concatenate([jnp.where(sub8 >= b, c0[:SUBS], x0), c0[SUBS:]], axis=0)
                c1 = jnp.concatenate([jnp.where(sub8 >= b, c1[:SUBS], x1), c1[SUBS:]], axis=0)
            return c0, c1

        def turn(p, i):
            r0 = pltpu.roll(shifted[b, p, i:i + chunk, :LANES], r, 1)
            r1 = pltpu.roll(shifted[b, p, i:i + chunk, LANES:], r, 1)
            return jnp.where(lane >= r, r0, r1), jnp.where(lane >= r, r1, r0)

        def wave(i):
            o_re, o_im = patch(0, i), patch(1, i)
            p_re, p_im = turn(0, i), turn(1, i)
            out = []
            for j in range(2):
                js = slice(j * LANES, (j + 1) * LANES)
                turned[0, i:i + chunk, js] = p_re[j]
                turned[1, i:i + chunk, js] = p_im[j]
                out.append((p_re[j] * o_re[j] - p_im[j] * o_im[j], p_re[j] * o_im[j] + p_im[j] * o_re[j]))
            return out

        for i in range(0, half, chunk):
            top, bot = wave(i), wave(i + half)
            for j in range(2):
                js = slice(j * LANES, (j + 1) * LANES)
                for c in range(2):
                    for e, v in enumerate((top[j][c] + bot[j][c], top[j][c] - bot[j][c])):
                        hi, lo = parts(v)
                        sh_h[e, c * half + i:c * half + i + chunk, js] = hi
                        sh_l[e, c * half + i:c * half + i + chunk, js] = lo
        mids = []
        for e in range(2):
            xh = sh_h[e]
            y = matmul(fr[e], jnp.concatenate([xh, xh, sh_l[e]], axis=0))
            mids.append((y[:half], y[half:]))
        far = []
        for sign in (1, -1):
            rows = []
            for re, im in mids:
                if sign == 1:
                    rows.append(jnp.concatenate([re[:, :half] + re[:, half:], im[:, :half] + im[:, half:]], axis=1))
                else:
                    rows.append(jnp.concatenate([re[:, :half] - re[:, half:], im[:, :half] - im[:, half:]], axis=1))
            x = jnp.concatenate(rows, axis=0)
            hi, lo = parts(x)
            far.append(matmul(jnp.concatenate([hi, hi, lo], axis=1), fc[0 if sign == 1 else 1]))
        m_rows = jnp.concatenate(
            [
                jnp.concatenate([meas[j, s, pl.ds(e, half, stride=2), :] for j in range(2)], axis=1)
                for e in range(2)
            ],
            axis=0,
        )
        m_hi, m_lo = parts(m_rows)
        amp = matmul(jnp.concatenate([m_hi, m_lo], axis=1), pick[...])
        total = jnp.zeros((SUBS, LANES), F32)
        backs = []
        for e in range(2):
            re, im = far[e][:, :half], far[e][:, half:]
            t = re * re + im * im + 1.0
            inv = lax.rsqrt(t)
            differ = t * inv - amp[:, e * half:(e + 1) * half]
            total = total + jnp.sum((differ * differ).reshape(extent // SUBS, SUBS, half), axis=0)
            factor = differ * inv
            z = jnp.concatenate([re * factor, im * factor], axis=1)
            hi, lo = parts(z)
            backs.append(matmul(jnp.concatenate([hi, hi, lo], axis=1), bc[e]))
        loss_out[s] = total
        left = backs[0] + backs[1]
        right = backs[0] - backs[1]
        outs = []
        for e in range(2):
            rs = slice(e * half, (e + 1) * half)
            x = jnp.concatenate(
                [
                    jnp.concatenate([left[rs, :half], right[rs, :half]], axis=1),
                    jnp.concatenate([left[rs, half:], right[rs, half:]], axis=1),
                ],
                axis=0,
            )
            hi, lo = parts(x)
            outs.append(matmul(br[e], jnp.concatenate([hi, hi, lo], axis=0)))
        for k, adj in enumerate((outs[0] + outs[1], outs[0] - outs[1])):
            for i0 in range(0, half, chunk):
                i = k * half + i0
                o_re, o_im = patch(0, i), patch(1, i)
                q_re, q_im = [], []
                for j in range(2):
                    js = slice(j * LANES, (j + 1) * LANES)
                    b_re = adj[i0:i0 + chunk, js]
                    b_im = adj[half + i0:half + i0 + chunk, js]
                    p_re, p_im = turned[0, i:i + chunk, js], turned[1, i:i + chunk, js]
                    g_re = p_re * b_re + p_im * b_im
                    g_im = p_re * b_im - p_im * b_re
                    q_re.append(o_re[j] * b_re + o_im[j] * b_im)
                    q_im.append(o_re[j] * b_im - o_im[j] * b_re)
                    for p, g in enumerate((g_re, g_im)):
                        if i == 0:
                            spill = jnp.where(sub8 < b, g[:SUBS], 0.0)
                            g = jnp.concatenate([jnp.where(sub8 >= b, g[:SUBS], 0.0), g[SUBS:]], axis=0)
                        if j == 0:
                            grad[p, at(i), cols[0]] += jnp.where(lane >= r, g, 0.0)
                            grad[p, at(i), cols[2]] += jnp.where(lane < r, g, 0.0)
                            if i == 0:
                                grad[p, at8(extent), cols[0]] += jnp.where(lane8 >= r, spill, 0.0)
                                grad[p, at8(extent), cols[2]] += jnp.where(lane8 < r, spill, 0.0)
                        else:
                            grad[p, at(i), cols[1]] += g
                            if i == 0:
                                grad[p, at8(extent), cols[1]] += spill
                back = lax.rem(LANES - r, LANES)
                for p, (h0, h1) in enumerate((q_re, q_im)):
                    h0 = pltpu.roll(h0, back, 1)
                    h1 = pltpu.roll(h1, back, 1)
                    keep = lane < LANES - r
                    accs[b, p, i:i + chunk, :LANES] += jnp.where(keep, h0, h1)
                    accs[b, p, i:i + chunk, LANES:] += jnp.where(keep, h1, h0)

    def step(s, c):
        row = centers[s, 0]
        col = centers[s, 1]
        inside = (row >= half) & (row <= tile - half) & (col >= half) & (col <= tile - half)
        wanted = inside if inner else jnp.logical_not(inside)

        @pl.when((live[s] > 0) & wanted)
        def _():
            visit(s)

        return c

    lax.fori_loop(0, slots, step, 0)

    stores = []

    def store(src, dst):
        stores.append(pltpu.make_async_copy(src, dst, sems.at[len(stores)]))
        stores[-1].start()

    if not inner:
        store(grad.at[:, :, pl.ds(0, half)], gleft)
        store(grad.at[:, :, pl.ds(half + tile, half)], gright)
        store(grad.at[:, pl.ds(0, half), mid], gup)
        store(grad.at[:, pl.ds(half + tile, half), mid], gdown)
    store(grad.at[:, mid, mid], grad_out)
    for p in range(2):
        acc = accs[0, p]
        for b in range(1, SUBS):
            acc = acc + pltpu.roll(accs[b, p], extent - b, 0)
        acc_out[p] = acc if inner else acc + acc_in[p]
    for c in stores:
        c.wait()


def run_slots(phase, centers, live, tile_obj, probe, measured, tables, extra=()):
    extent = probe.shape[1]
    half = extent // 2
    slots = centers.shape[0]
    tile = tile_obj.shape[1]
    size = tile + 2 * half
    inner = phase == "inner"
    smem = pl.BlockSpec(memory_space=pltpu.SMEM)
    hbm = pl.BlockSpec(memory_space=pl.ANY)
    vmem = pl.BlockSpec(memory_space=pltpu.VMEM)
    in_specs = [smem, smem, hbm, vmem, hbm] + [vmem] * 5
    out_shape = [
        jax.ShapeDtypeStruct((2, tile, tile), F32),
        jax.ShapeDtypeStruct((2, extent, extent), F32),
        jax.ShapeDtypeStruct((slots, SUBS, LANES), F32),
    ]
    out_specs = [hbm, vmem, vmem]
    if not inner:
        in_specs += [hbm] * 6 + [vmem, vmem]
        out_shape += [jax.ShapeDtypeStruct((2, half, tile), F32)] * 2
        out_shape += [jax.ShapeDtypeStruct((2, size, half), F32)] * 2
        out_specs += [hbm] * 4
    flops = slots * 16 * 2 * extent**3
    return pl.pallas_call(
        functools.partial(slot_kernel, phase, extent, slots, tile),
        out_shape=out_shape,
        in_specs=in_specs,
        out_specs=out_specs,
        scratch_shapes=[
            pltpu.VMEM((2, size, size), F32),
            pltpu.VMEM((2, size, size), F32),
            pltpu.VMEM((SUBS, 2, extent, extent), F32),
            pltpu.VMEM((SUBS, 2, extent, extent), F32),
            pltpu.VMEM((2, extent, extent), F32),
            pltpu.VMEM((2, slots, extent, LANES), F32),
            pltpu.VMEM((2, extent, extent), BF),
            pltpu.VMEM((2, extent, extent), BF),
            pltpu.SemaphoreType.DMA((12,)),
            pltpu.SemaphoreType.DMA((2,)),
        ],
        compiler_params=pltpu.CompilerParams(vmem_limit_bytes=60 * 2**20),
        cost_estimate=pl.CostEstimate(flops=flops, bytes_accessed=32 * 2**20, transcendentals=0),
        name="slots_" + phase,
    )(centers, live, tile_obj, probe, measured, *tables, *extra)


def shift(x, axis, up):
    n = lax.axis_size(axis)
    if up:
        return lax.ppermute(x, axis, [(i, i + 1) for i in range(n - 1)])
    return lax.ppermute(x, axis, [(i + 1, i) for i in range(n - 1)])


def sum_all(x, axes):
    flat = x.reshape(-1, LANES)

    def scatter(y, axis):
        n = lax.axis_size(axis)
        me = lax.axis_index(axis)
        rows = y.shape[0] // n
        own = lax.dynamic_slice_in_dim(y, me * rows, rows, 0)
        got = []
        for k in range(1, n):
            piece = lax.dynamic_slice_in_dim(y, lax.rem(me + k, n) * rows, rows, 0)
            got.append(lax.ppermute(piece, axis, [(i, (i + k) % n) for i in range(n)]))
        for piece in got:
            own = own + piece
        return own

    def gather(y, axis):
        n = lax.axis_size(axis)
        me = lax.axis_index(axis)
        rows = y.shape[0]
        out = jnp.zeros((n * rows,) + y.shape[1:], y.dtype)
        out = lax.dynamic_update_slice_in_dim(out, y, me * rows, 0)
        for k in range(1, n):
            piece = lax.ppermute(y, axis, [(i, (i + k) % n) for i in range(n)])
            out = lax.dynamic_update_slice_in_dim(out, piece, lax.rem(me + n - k, n) * rows, 0)
        return out

    for axis in axes:
        flat = scatter(flat, axis)
    for axis in reversed(axes):
        flat = gather(flat, axis)
    return flat.reshape(x.shape)


def on_device(object_field, probe, centers, live, measured):
    extent = probe.shape[1]
    half = extent // 2
    tile = object_field.shape[1]
    slots = centers.shape[0]
    tables = [jnp.asarray(t) for t in tables_np(extent)]

    up = shift(object_field[:, tile - half:, :], "gx", True)
    down = shift(object_field[:, :half, :], "gx", False)
    left = shift(object_field[:, :, tile - half:], "gy", True)
    right = shift(object_field[:, :, :half], "gy", False)
    ends = jnp.stack([up, down])
    corner_l = shift(ends[:, :, :, tile - half:], "gy", True)
    corner_r = shift(ends[:, :, :, :half], "gy", False)
    corners = jnp.stack([corner_l, corner_r])

    grad_a, acc_a, loss_a = run_slots("inner", centers, live, object_field, probe, measured, tables)
    grad_b, acc_b, loss_b, gup, gdown, gleft, gright = run_slots(
        "outer", centers, live, object_field, probe, measured, tables,
        (up, down, left, right, corners, grad_a, acc_a, loss_a),
    )
    from_left = shift(gright, "gy", True)
    from_right = shift(gleft, "gy", False)
    from_up = shift(gdown, "gx", True)
    from_down = shift(gup, "gx", False)
    bottoms = jnp.stack([from_left[:, half + tile:, :], from_right[:, half + tile:, :]])
    tops = jnp.stack([from_left[:, :half, :], from_right[:, :half, :]])
    corner_up = shift(bottoms, "gx", True)
    corner_down = shift(tops, "gx", False)
    totals = sum_all(acc_b, ("gx", "gy"))

    top_add = from_up.at[:, :, :half].add(corner_up[0]).at[:, :, tile - half:].add(corner_up[1])
    bot_add = from_down.at[:, :, :half].add(corner_down[0]).at[:, :, tile - half:].add(corner_down[1])
    out = grad_b
    out = out.at[:, :, :half].add(from_left[:, half:half + tile, :])
    out = out.at[:, :, tile - half:].add(from_right[:, half:half + tile, :])
    out = out.at[:, :half, :].add(top_add)
    out = out.at[:, tile - half:, :].add(bot_add)

    slots_all = slots * lax.axis_size("gx") * lax.axis_size("gy")
    probe_grad = totals / math.sqrt(slots_all)
    slot_loss = jnp.sum(loss_b, axis=(1, 2)) * (0.5 / (extent * extent))
    return out, probe_grad, slot_loss


def solution(mesh):
    placed = (
        P(None, "gx", "gy"),
        P(),
        P(("gx", "gy"), None),
        P(("gx", "gy")),
        P(("gx", "gy"), None, None),
    )
    return jax.shard_map(
        on_device,
        mesh=mesh,
        in_specs=placed,
        out_specs=(P(None, "gx", "gy"), P(), P(("gx", "gy"))),
        check_vma=False,
    )
```

```python
import functools
import math

import jax
import jax.numpy as jnp
import numpy as np
from jax import lax
from jax.experimental import pallas as pl
from jax.experimental.pallas import tpu as pltpu
from jax.sharding import PartitionSpec as P


LANES = 128
SUBS = 8
PLAN = "bfbfbfbfbfbfbfbfbfbfbfb"
BF = jnp.bfloat16
F32 = jnp.float32


def split_np(table):
    hi = table.astype(np.float32).astype(jnp.bfloat16)
    lo = (table - hi.astype(np.float64)).astype(np.float32).astype(jnp.bfloat16)
    return hi, lo


def tables_np(extent):
    half = extent // 2
    k = np.arange(extent)[:, None]
    n = np.arange(half)[None, :]
    angle = -2.0 * np.pi * ((k * n) % extent) / extent
    re = np.cos(angle) / math.sqrt(extent)
    im = np.sin(angle) / math.sqrt(extent)
    mats = []
    for parity in range(2):
        a, b = re[parity::2], im[parity::2]
        left = np.block([[a, -b], [b, a]])
        mats += [np.stack(split_np(left)), np.stack(split_np(left.T))]
    pick = np.zeros((extent, extent), np.float32)
    pick[2 * np.arange(half), np.arange(half)] = 1
    pick[2 * np.arange(half) + 1, half + np.arange(half)] = 1
    return np.stack(mats), pick.astype(jnp.bfloat16)


def parts(x):
    hi = x.astype(BF)
    lo = (x - hi.astype(F32)).astype(BF)
    return hi, lo


def matmul(a, b):
    return jnp.dot(a, b, preferred_element_type=F32)


def slot_kernel(
    phase, extent, slots, tile,
    centers, live, *refs,
):
    half = extent // 2
    inner = phase == "inner"
    it = iter(refs)
    take = lambda n: [next(it) for _ in range(n)]
    tile_hbm, probe, meas_hbm, mats, pick = take(5)
    if not inner:
        sides_hbm, corners_hbm = take(4), take(4)
        grad_in, acc_in, loss_in = take(3)
        del grad_in
    grad_out, acc_out, loss_out = take(3)
    if not inner:
        gsides, gcorners = take(4), take(4)
    ext, grad, shifted, accs, turned, kept, meas, sh_h, sh_l, z_h, z_l, sems, msems, order = take(14)
    mid = pl.ds(half, tile)
    low, high = pl.ds(0, half), pl.ds(half + tile, half)
    sides = ((low, mid), (high, mid), (mid, low), (mid, high))
    corners = ((low, low), (low, high), (high, low), (high, high))
    band = min(extent, tile // 2)
    rest = tile - 2 * band
    ring = [(0, band, 0, tile), (tile - band, band, 0, tile)]
    if rest:
        ring += [(band, rest, 0, band), (band, rest, tile - band, band)]

    copies = []

    def copy(src, dst):
        copies.append(pltpu.make_async_copy(src, dst, sems.at[len(copies)]))
        copies[-1].start()

    def own(ref, box, shift):
        return ref.at[:, pl.ds(box[0] + shift, box[1]), pl.ds(box[2] + shift, box[3])]

    def wanted(s):
        row = centers[s, 0]
        col = centers[s, 1]
        inside = (row >= half) & (row <= tile - half) & (col >= half) & (col <= tile - half)
        return (live[s] > 0) & (inside if inner else jnp.logical_not(inside))

    def fetch(s, j):
        return pltpu.make_async_copy(meas_hbm.at[s, :, pl.ds(j * LANES, LANES)], meas.at[j, s], msems.at[j, s])

    if inner:
        copy(tile_hbm, ext.at[:, mid, mid])
    else:
        for src, (rows, cols) in zip(sides_hbm + corners_hbm, sides + corners):
            copy(src, ext.at[:, rows, cols])
        for box in ring:
            copy(own(tile_hbm, box, 0), own(ext, box, half))
    loads = list(copies)

    def prefetch(s, n):
        go = wanted(s)
        order[n] = s

        @pl.when(go)
        def _():
            for j in range(2):
                fetch(s, j).start()

        return n + go.astype(jnp.int32)

    count = lax.fori_loop(0, slots, prefetch, jnp.int32(0))
    if not inner:
        for box in ring:
            copy(own(grad_out, box, 0), own(grad, box, half))
    late = copies[len(loads):]

    for p in range(2):
        plane = probe[p]
        for b in range(SUBS):
            shifted[b, p] = pltpu.roll(plane, b, 0) if b else plane
    accs[...] = jnp.zeros_like(accs)
    step_rows = 4 * SUBS

    def clear(rows, cols):
        block = jnp.zeros((2, step_rows, cols.size), F32)

        def body(i, c):
            at = pl.multiple_of(rows.start + i * step_rows, step_rows)
            grad[:, pl.ds(at, step_rows), cols] = block
            return c

        lax.fori_loop(0, rows.size // step_rows, body, 0)

    if inner:
        loss_out[...] = jnp.zeros_like(loss_out)
        clear(mid, mid)
    else:
        loss_out[...] = loss_in[...]
        for rows, cols in sides + corners:
            clear(rows, cols)
    for c in loads:
        c.wait()

    chunk = 32
    lane8 = lax.broadcasted_iota(jnp.int32, (SUBS, LANES), 1)
    sub8 = lax.broadcasted_iota(jnp.int32, (SUBS, LANES), 0)

    lane = lax.broadcasted_iota(jnp.int32, (chunk, LANES), 1)

    def place(s):
        row, col = centers[s, 0], centers[s, 1]
        b, r = lax.rem(row, SUBS), lax.rem(col, LANES)
        a8, q = row - b, col - r
        cols = [pl.ds(pl.multiple_of(q + j * LANES, LANES), LANES) for j in range(3)]
        at = lambda off: pl.ds(pl.multiple_of(a8 + off, SUBS), chunk)
        at8 = pl.ds(pl.multiple_of(a8 + extent, SUBS), SUBS)
        return b, r, cols, at, at8

    def patch(where, p, i):
        b, r, cols, at, at8 = where
        c0 = jnp.where(lane >= r, ext[p, at(i), cols[0]], ext[p, at(i), cols[2]])
        c1 = ext[p, at(i), cols[1]]
        if i == 0:
            x0 = jnp.where(lane8 >= r, ext[p, at8, cols[0]], ext[p, at8, cols[2]])
            x1 = ext[p, at8, cols[1]]
            c0 = jnp.concatenate([jnp.where(sub8 >= b, c0[:SUBS], x0), c0[SUBS:]], axis=0)
            c1 = jnp.concatenate([jnp.where(sub8 >= b, c1[:SUBS], x1), c1[SUBS:]], axis=0)
        return c0, c1

    def left_mul(m, hi, lo):
        table = jnp.concatenate([mats[m, 0], mats[m, 1], mats[m, 0]], axis=1)
        return matmul(table, jnp.concatenate([hi, hi, lo], axis=0))

    def right_mul(hi, lo, m):
        table = jnp.concatenate([mats[m, 0], mats[m, 1], mats[m, 0]], axis=0)
        return matmul(jnp.concatenate([hi, hi, lo], axis=1), table)

    def front(s):
        where = place(s)
        b, r = where[:2]

        def turn(p, i):
            r0 = pltpu.roll(shifted[b, p, i:i + chunk, :LANES], r, 1)
            r1 = pltpu.roll(shifted[b, p, i:i + chunk, LANES:], r, 1)
            return jnp.where(lane >= r, r0, r1), jnp.where(lane >= r, r1, r0)

        def wave(i):
            o_re, o_im = patch(where, 0, i), patch(where, 1, i)
            p_re, p_im = turn(0, i), turn(1, i)
            out = []
            for j in range(2):
                js = slice(j * LANES, (j + 1) * LANES)
                turned[0, i:i + chunk, js] = p_re[j]
                turned[1, i:i + chunk, js] = p_im[j]
                out.append((p_re[j] * o_re[j] - p_im[j] * o_im[j], p_re[j] * o_im[j] + p_im[j] * o_re[j]))
            return out

        for i in range(0, half, chunk):
            top, bot = wave(i), wave(i + half)
            for j in range(2):
                js = slice(j * LANES, (j + 1) * LANES)
                for c in range(2):
                    for e, v in enumerate((top[j][c] + bot[j][c], top[j][c] - bot[j][c])):
                        hi, lo = parts(v)
                        sh_h[e, c * half + i:c * half + i + chunk, js] = hi
                        sh_l[e, c * half + i:c * half + i + chunk, js] = lo
            yield
        mids = []
        for e in range(2):
            y = left_mul(2 * e, sh_h[e], sh_l[e])
            mids.append((y[:half], y[half:]))
            yield
        far = []
        for e in range(2):
            rows = []
            for re, im in mids:
                if e == 0:
                    halves = [re[:, :half] + re[:, half:], im[:, :half] + im[:, half:]]
                else:
                    halves = [re[:, :half] - re[:, half:], im[:, :half] - im[:, half:]]
                rows.append(jnp.concatenate(halves, axis=1))
            hi, lo = parts(jnp.concatenate(rows, axis=0))
            far.append(right_mul(hi, lo, 2 * e + 1))
            yield
        m_rows = jnp.concatenate(
            [
                jnp.concatenate([meas[j, s, pl.ds(e, half, stride=2), :] for j in range(2)], axis=1)
                for e in range(2)
            ],
            axis=0,
        )
        m_hi, m_lo = parts(m_rows)
        amp = matmul(jnp.concatenate([m_hi, m_lo], axis=1), jnp.concatenate([pick[...]] * 2, axis=0))
        yield
        total = jnp.zeros((SUBS, LANES), F32)
        for e in range(2):
            re, im = far[e][:, :half], far[e][:, half:]
            t = re * re + im * im + 1.0
            inv = lax.rsqrt(t)
            differ = t * inv - amp[:, e * half:(e + 1) * half]
            total = total + jnp.sum((differ * differ).reshape(extent // SUBS, SUBS, half), axis=0)
            factor = differ * inv
            hi, lo = parts(jnp.concatenate([re * factor, im * factor], axis=1))
            z_h[e] = hi
            z_l[e] = lo
            yield
        loss_out[s] = total

    def back(s):
        where = place(s)
        b, r, cols, at, at8 = where
        backs = []
        for e in range(2):
            backs.append(right_mul(z_h[e], z_l[e], 2 * e))
            yield
        outs = []
        for e in range(2):
            rs = slice(e * half, (e + 1) * half)
            left, right = backs[0][rs] + backs[1][rs], backs[0][rs] - backs[1][rs]
            x = jnp.concatenate(
                [
                    jnp.concatenate([left[:, :half], right[:, :half]], axis=1),
                    jnp.concatenate([left[:, half:], right[:, half:]], axis=1),
                ],
                axis=0,
            )
            hi, lo = parts(x)
            outs.append(left_mul(2 * e + 1, hi, lo))
            yield
        for k in range(2):
            for i0 in range(0, half, chunk):
                i = k * half + i0
                o_re, o_im = patch(where, 0, i), patch(where, 1, i)
                q_re, q_im = [], []
                for j in range(2):
                    js = slice(j * LANES, (j + 1) * LANES)
                    pair = [(outs[0][at0:at0 + chunk, js], outs[1][at0:at0 + chunk, js]) for at0 in (i0, half + i0)]
                    b_re, b_im = [(u + v) if k == 0 else (u - v) for u, v in pair]
                    p_re, p_im = kept[0, i:i + chunk, js], kept[1, i:i + chunk, js]
                    g_re = p_re * b_re + p_im * b_im
                    g_im = p_re * b_im - p_im * b_re
                    q_re.append(o_re[j] * b_re + o_im[j] * b_im)
                    q_im.append(o_re[j] * b_im - o_im[j] * b_re)
                    for p, g in enumerate((g_re, g_im)):
                        if i == 0:
                            spill = jnp.where(sub8 < b, g[:SUBS], 0.0)
                            g = jnp.concatenate([jnp.where(sub8 >= b, g[:SUBS], 0.0), g[SUBS:]], axis=0)
                        if j == 0:
                            grad[p, at(i), cols[0]] += jnp.where(lane >= r, g, 0.0)
                            grad[p, at(i), cols[2]] += jnp.where(lane < r, g, 0.0)
                            if i == 0:
                                grad[p, at8, cols[0]] += jnp.where(lane8 >= r, spill, 0.0)
                                grad[p, at8, cols[2]] += jnp.where(lane8 < r, spill, 0.0)
                        else:
                            grad[p, at(i), cols[1]] += g
                            if i == 0:
                                grad[p, at8, cols[1]] += spill
                turn_back = lax.rem(LANES - r, LANES)
                for p, (h0, h1) in enumerate((q_re, q_im)):
                    h0 = pltpu.roll(h0, turn_back, 1)
                    h1 = pltpu.roll(h1, turn_back, 1)
                    keep = lane < LANES - r
                    accs[b, p, i:i + chunk, :LANES] += jnp.where(keep, h0, h1)
                    accs[b, p, i:i + chunk, LANES:] += jnp.where(keep, h1, h0)
                yield

    def run(streams, plan=""):
        left = dict(streams)
        for name in plan:
            next(left[name])
        for stream in left.values():
            for _ in stream:
                pass

    def keep_probe():
        for p in range(2):
            kept[p] = turned[p]

    def ready(s):
        for j in range(2):
            fetch(s, j).wait()

    @pl.when(count > 0)
    def _():
        ready(order[0])
        run({"f": front(order[0])})
        keep_probe()

    for c in late:
        c.wait()

    def step(t, c):
        ready(order[t])
        run({"b": back(order[t - 1]), "f": front(order[t])}, PLAN)
        keep_probe()
        return c

    lax.fori_loop(1, count, step, 0)

    @pl.when(count > 0)
    def _():
        run({"b": back(order[count - 1])})

    copies.clear()
    if inner:
        copy(grad.at[:, mid, mid], grad_out)
    else:
        for dst, (rows, cols) in zip(gsides + gcorners, sides + corners):
            copy(grad.at[:, rows, cols], dst)
        for box in ring:
            copy(own(grad, box, half), own(grad_out, box, 0))
    for p in range(2):
        acc = accs[0, p]
        for b in range(1, SUBS):
            acc = acc + pltpu.roll(accs[b, p], extent - b, 0)
        for j in range(extent // LANES):
            at = pl.ds((p * (extent // LANES) + j) * extent, extent)
            part = acc[:, j * LANES:(j + 1) * LANES]
            acc_out[at, :] = part if inner else part + acc_in[at, :]
    for c in copies:
        c.wait()


def run_slots(phase, centers, live, tile_obj, probe, measured, tables, extra=()):
    extent = probe.shape[1]
    half = extent // 2
    slots = centers.shape[0]
    tile = tile_obj.shape[1]
    size = tile + 2 * half
    inner = phase == "inner"
    smem = pl.BlockSpec(memory_space=pltpu.SMEM)
    hbm = pl.BlockSpec(memory_space=pl.ANY)
    vmem = pl.BlockSpec(memory_space=pltpu.VMEM)
    in_specs = [smem, smem, hbm, vmem, hbm, vmem, vmem]
    out_shape = [
        jax.ShapeDtypeStruct((2, tile, tile), F32),
        jax.ShapeDtypeStruct((2 * extent * extent // LANES, LANES), F32),
        jax.ShapeDtypeStruct((slots, SUBS, LANES), F32),
    ]
    out_specs = [hbm, vmem, vmem]
    if not inner:
        in_specs += [hbm] * 9 + [vmem, vmem]
        out_shape += [jax.ShapeDtypeStruct((2, half, tile), F32)] * 2
        out_shape += [jax.ShapeDtypeStruct((2, tile, half), F32)] * 2
        out_shape += [jax.ShapeDtypeStruct((2, half, half), F32)] * 4
        out_specs += [hbm] * 8
    flops = slots * 16 * 2 * extent**3
    return pl.pallas_call(
        functools.partial(slot_kernel, phase, extent, slots, tile),
        out_shape=out_shape,
        in_specs=in_specs,
        out_specs=out_specs,
        scratch_shapes=[
            pltpu.VMEM((2, size, size), F32),
            pltpu.VMEM((2, size, size), F32),
            pltpu.VMEM((SUBS, 2, extent, extent), F32),
            pltpu.VMEM((SUBS, 2, extent, extent), F32),
            pltpu.VMEM((2, extent, extent), F32),
            pltpu.VMEM((2, extent, extent), F32),
            pltpu.VMEM((2, slots, extent, LANES), F32),
            pltpu.VMEM((2, extent, extent), BF),
            pltpu.VMEM((2, extent, extent), BF),
            pltpu.VMEM((2, extent, extent), BF),
            pltpu.VMEM((2, extent, extent), BF),
            pltpu.SemaphoreType.DMA((16,)),
            pltpu.SemaphoreType.DMA((2, slots)),
            pltpu.SMEM((slots + 1,), jnp.int32),
        ],
        compiler_params=pltpu.CompilerParams(vmem_limit_bytes=60 * 2**20),
        cost_estimate=pl.CostEstimate(flops=flops, bytes_accessed=32 * 2**20, transcendentals=0),
        input_output_aliases={} if inner else {len(in_specs) - 3: 0},
    )(centers, live, tile_obj, probe, measured, *tables, *extra)


def sum_all(x, groups, scale, shape):
    flat = x

    def send(y, axis, stride, count, k):
        n = lax.axis_size(axis)
        spot = lambda i: (i // stride) % count
        pairs = [(i, i + ((spot(i) + k) % count - spot(i)) * stride) for i in range(n)]
        return lax.ppermute(y, axis, pairs)

    def place(axis, stride, count):
        return lax.rem(lax.axis_index(axis) // stride, count)

    for axis, stride, count in groups:
        me = place(axis, stride, count)
        rows = flat.shape[0] // count
        own = lax.dynamic_slice_in_dim(flat, me * rows, rows, 0)
        got = [
            send(lax.dynamic_slice_in_dim(flat, lax.rem(me + k, count) * rows, rows, 0), axis, stride, count, k)
            for k in range(1, count)
        ]
        flat = sum(got, own)
    for level, (axis, stride, count) in reversed(list(enumerate(groups))):
        pieces = [flat] + [send(flat, axis, stride, count, k) for k in range(1, count)]
        me = place(axis, stride, count)
        if level == 0 and count == 2:
            return finish(me, pieces, scale, shape)
        rows = flat.shape[0]
        out = jnp.zeros((count * rows, LANES), F32)
        for k, piece in enumerate(pieces):
            out = lax.dynamic_update_slice_in_dim(out, piece, lax.rem(me + count - k, count) * rows, 0)
        flat = out
    return finish(jnp.int32(0), [flat], scale, shape)


def finish_kernel(scale, me, *refs):
    pieces, out = refs[:-1], refs[-1]
    planes, extent, width = out.shape
    each = planes // len(pieces)
    for k, piece in enumerate(pieces):
        owner = me[0] if k == 0 else len(pieces) - 1 - me[0]
        for p in range(each):
            for j in range(width // LANES):
                at = (p * (width // LANES) + j) * extent
                out[owner * each + p, :, j * LANES:(j + 1) * LANES] = piece[at:at + extent, :] * scale


def finish(me, pieces, scale, shape):
    vmem = pl.BlockSpec(memory_space=pltpu.VMEM)
    return pl.pallas_call(
        functools.partial(finish_kernel, scale),
        out_shape=jax.ShapeDtypeStruct(shape, F32),
        in_specs=[pl.BlockSpec(memory_space=pltpu.SMEM)] + [vmem] * len(pieces),
        out_specs=vmem,
        compiler_params=pltpu.CompilerParams(vmem_limit_bytes=8 * 2**20),
        cost_estimate=pl.CostEstimate(flops=2**17, bytes_accessed=2**20, transcendentals=0),
        name="finish",
    )(me.reshape(1), *pieces)


def sum_groups():
    nx, ny = lax.axis_size("gx"), lax.axis_size("gy")
    groups = [("gx", 1, 2), ("gx", 2, nx // 2)] if nx % 2 == 0 else [("gx", 1, nx)]
    return [g for g in groups + [("gy", 1, ny)] if g[2] > 1]


def fold_kernel(half, tile, main, *refs):
    adds, corners = refs[:4], refs[4:8]
    out, rows_buf, cols_buf, rows_add, cols_add, corner_add, sems = refs[8:]
    del main
    inside = tile - 2 * half
    copies = []

    def copy(src, dst):
        copies.append(pltpu.make_async_copy(src, dst, sems.at[len(copies)]))
        copies[-1].start()

    far = tile - half
    rows_at = [out.at[:, pl.ds(r, half), :] for r in (0, far)]
    cols_at = [out.at[:, pl.ds(half, inside), pl.ds(c, half)] for c in (0, far)]
    for k in range(2):
        copy(rows_at[k], rows_buf.at[k])
        copy(adds[k], rows_add.at[k])
        copy(cols_at[k], cols_buf.at[k])
        copy(adds[2 + k], cols_add.at[k])
    for k in range(4):
        copy(corners[k], corner_add.at[k])
    for c in copies:
        c.wait()
    copies.clear()
    step = 4 * SUBS
    for k in range(2):
        def rows_body(i, c, k=k):
            at = pl.ds(pl.multiple_of(i * step, step), step)
            side_at = pl.ds(pl.multiple_of(i * step + k * far, step), step)
            for p in range(2):
                rows_buf[k, p, at, :] += rows_add[k, p, at, :]
                for j, c0 in enumerate((0, far)):
                    lanes = slice(c0, c0 + half)
                    rows_buf[k, p, at, lanes] += cols_add[j, p, side_at, :] + corner_add[2 * k + j, p, at, :]
            return c

        lax.fori_loop(0, half // step, rows_body, 0)
        copy(rows_buf.at[k], rows_at[k])

        def cols_body(i, c, k=k):
            at = pl.ds(pl.multiple_of(i * step, step), step)
            side_at = pl.ds(pl.multiple_of(half + i * step, step), step)
            for p in range(2):
                cols_buf[k, p, at, :] += cols_add[k, p, side_at, :]
            return c

        lax.fori_loop(0, inside // step, cols_body, 0)
        copy(cols_buf.at[k], cols_at[k])
    for c in copies:
        c.wait()


def fold(main, adds, corners):
    tile = main.shape[1]
    half = adds[0].shape[1]
    hbm = pl.BlockSpec(memory_space=pl.ANY)
    return pl.pallas_call(
        functools.partial(fold_kernel, half, tile),
        out_shape=jax.ShapeDtypeStruct(main.shape, F32),
        in_specs=[hbm] * 9,
        out_specs=hbm,
        scratch_shapes=[
            pltpu.VMEM((2, 2, half, tile), F32),
            pltpu.VMEM((2, 2, tile - 2 * half, half), F32),
            pltpu.VMEM((2, 2, half, tile), F32),
            pltpu.VMEM((2, 2, tile, half), F32),
            pltpu.VMEM((4, 2, half, half), F32),
            pltpu.SemaphoreType.DMA((12,)),
        ],
        input_output_aliases={0: 0},
        compiler_params=pltpu.CompilerParams(vmem_limit_bytes=24 * 2**20),
        cost_estimate=pl.CostEstimate(flops=2**21, bytes_accessed=14 * 2**20, transcendentals=0),
        name="fold",
    )(main, *adds, *corners)


def shift2(x, dx, dy):
    nx, ny = lax.axis_size("gx"), lax.axis_size("gy")
    pairs = [
        (i * ny + j, (i + dx) * ny + j + dy)
        for i in range(nx)
        for j in range(ny)
        if 0 <= i + dx < nx and 0 <= j + dy < ny
    ]
    return lax.ppermute(x, ("gx", "gy"), pairs)


SIDES = ((1, 0), (-1, 0), (0, 1), (0, -1))
CORNERS = ((1, 1), (1, -1), (-1, 1), (-1, -1))


def on_device(object_field, probe, centers, live, measured):
    extent = probe.shape[1]
    half = extent // 2
    tile = object_field.shape[1]
    slots = centers.shape[0]
    tables = [jnp.asarray(t) for t in tables_np(extent)]
    far = tile - half

    def end(step):
        if step == 0:
            return slice(None)
        return slice(far, tile) if step == 1 else slice(0, half)

    def bring(dx, dy):
        return shift2(object_field[:, end(dx), end(dy)], dx, dy)

    left, right = bring(0, 1), bring(0, -1)
    up, down = bring(1, 0), bring(-1, 0)

    corners = [bring(dx, dy) for dx, dy in CORNERS]
    grad_a, acc_a, loss_a = run_slots("inner", centers, live, object_field, probe, measured, tables)
    out = run_slots(
        "outer", centers, live, object_field, probe, measured, tables,
        (up, down, left, right, *corners, grad_a, acc_a, loss_a),
    )
    grad_b, acc_b, loss_b = out[:3]
    sent = {}
    for places in ((2, 3), (0, 1), (4, 5, 6, 7)):
        for k in places:
            dx, dy = (SIDES + CORNERS)[k]
            sent[k] = shift2(out[3 + k], -dx, -dy)
    sides = [sent[1], sent[0], sent[3], sent[2]]
    corners = [sent[7], sent[6], sent[5], sent[4]]
    slots_all = slots * lax.axis_size("gx") * lax.axis_size("gy")
    probe_grad = sum_all(acc_b, sum_groups(), 1.0 / math.sqrt(slots_all), probe.shape)
    object_grad = fold(grad_b, sides, corners)

    slot_loss = jnp.sum(loss_b, axis=(1, 2)) * (0.5 / (extent * extent))
    return object_grad, probe_grad, slot_loss


def solution(mesh):
    placed = (
        P(None, "gx", "gy"),
        P(),
        P(("gx", "gy"), None),
        P(("gx", "gy")),
        P(("gx", "gy"), None, None),
    )
    return jax.shard_map(
        on_device,
        mesh=mesh,
        in_specs=placed,
        out_specs=(P(None, "gx", "gy"), P(), P(("gx", "gy"))),
        check_vma=False,
    )
```

```python
import functools
import math

import jax
import jax.numpy as jnp
import numpy as np
from jax import lax
from jax.experimental import pallas as pl
from jax.experimental.pallas import tpu as pltpu
from jax.sharding import PartitionSpec as P


LANES = 128
SUBS = 8
PLAN = "bfbfbfbfbfbfbfbfbfbfbfb"
BF = jnp.bfloat16
F32 = jnp.float32


def split_np(table):
    hi = table.astype(np.float32).astype(jnp.bfloat16)
    lo = (table - hi.astype(np.float64)).astype(np.float32).astype(jnp.bfloat16)
    return hi, lo


def tables_np(extent):
    half = extent // 2
    k = np.arange(extent)[:, None]
    n = np.arange(half)[None, :]
    angle = -2.0 * np.pi * ((k * n) % extent) / extent
    re = np.cos(angle) / math.sqrt(extent)
    im = np.sin(angle) / math.sqrt(extent)
    mats = []
    for parity in range(2):
        a, b = re[parity::2], im[parity::2]
        left = np.block([[a, -b], [b, a]])
        mats += [np.stack(split_np(left)), np.stack(split_np(left.T))]
    pick = np.zeros((extent, extent), np.float32)
    pick[2 * np.arange(half), np.arange(half)] = 1
    pick[2 * np.arange(half) + 1, half + np.arange(half)] = 1
    return np.stack(mats), pick.astype(jnp.bfloat16)


def parts(x):
    hi = x.astype(BF)
    lo = (x - hi.astype(F32)).astype(BF)
    return hi, lo


def matmul(a, b):
    return jnp.dot(a, b, preferred_element_type=F32)


def slot_kernel(
    phase, extent, slots, tile,
    centers, live, *refs,
):
    half = extent // 2
    inner = phase == "inner"
    it = iter(refs)
    take = lambda n: [next(it) for _ in range(n)]
    tile_hbm, probe, meas_hbm, mats, pick = take(5)
    if not inner:
        sides_hbm = take(4)
        grad_in, acc_in, loss_in = take(3)
        del grad_in
    grad_out, acc_out, loss_out = take(3)
    if not inner:
        gsides = take(8)
    ext, grad, shifted, accs, turned, kept, meas, sh_h, sh_l, z_h, z_l, sems, msems, order = take(14)
    mid = pl.ds(half, tile)
    low, high = pl.ds(0, half), pl.ds(half + tile, half)
    whole = pl.ds(0, 2 * half + tile)
    sides_in = ((low, whole), (high, whole), (mid, low), (mid, high))
    sides_out = ((low, mid), (high, mid), (mid, low), (mid, high))
    sides_out += ((low, low), (low, high), (high, low), (high, high))
    band = min(extent, tile // 2)
    rest = tile - 2 * band
    ring = [(0, band, 0, tile), (tile - band, band, 0, tile)]
    if rest:
        ring += [(band, rest, 0, band), (band, rest, tile - band, band)]

    copies = []

    def copy(src, dst):
        copies.append(pltpu.make_async_copy(src, dst, sems.at[len(copies)]))
        copies[-1].start()

    def own(ref, box, shift):
        return ref.at[:, pl.ds(box[0] + shift, box[1]), pl.ds(box[2] + shift, box[3])]

    def wanted(s):
        row = centers[s, 0]
        col = centers[s, 1]
        inside = (row >= half) & (row <= tile - half) & (col >= half) & (col <= tile - half)
        return (live[s] > 0) & (inside if inner else jnp.logical_not(inside))

    def fetch(s, j):
        return pltpu.make_async_copy(meas_hbm.at[s, :, pl.ds(j * LANES, LANES)], meas.at[j, s], msems.at[j, s])

    if inner:
        copy(tile_hbm, ext.at[:, mid, mid])
    else:
        for src, (rows, cols) in zip(sides_hbm, sides_in):
            copy(src, ext.at[:, rows, cols])
        for box in ring:
            copy(own(tile_hbm, box, 0), own(ext, box, half))
    loads = list(copies)

    def prefetch(s, n):
        go = wanted(s)
        order[n] = s

        @pl.when(go)
        def _():
            for j in range(2):
                fetch(s, j).start()

        return n + go.astype(jnp.int32)

    count = lax.fori_loop(0, slots, prefetch, jnp.int32(0))
    if not inner:
        for box in ring:
            copy(own(grad_out, box, 0), own(grad, box, half))
    late = copies[len(loads):]

    for p in range(2):
        plane = probe[p]
        for b in range(SUBS):
            shifted[b, p] = pltpu.roll(plane, b, 0) if b else plane
    accs[...] = jnp.zeros_like(accs)
    step_rows = 4 * SUBS

    def clear(rows, cols):
        block = jnp.zeros((2, step_rows, cols.size), F32)

        def body(i, c):
            at = pl.multiple_of(rows.start + i * step_rows, step_rows)
            grad[:, pl.ds(at, step_rows), cols] = block
            return c

        lax.fori_loop(0, rows.size // step_rows, body, 0)

    if inner:
        loss_out[...] = jnp.zeros_like(loss_out)
        clear(mid, mid)
    else:
        loss_out[...] = loss_in[...]
        for rows, cols in sides_in:
            clear(rows, cols)
    for c in loads:
        c.wait()

    chunk = 32
    lane8 = lax.broadcasted_iota(jnp.int32, (SUBS, LANES), 1)
    sub8 = lax.broadcasted_iota(jnp.int32, (SUBS, LANES), 0)

    lane = lax.broadcasted_iota(jnp.int32, (chunk, LANES), 1)

    def place(s):
        row, col = centers[s, 0], centers[s, 1]
        b, r = lax.rem(row, SUBS), lax.rem(col, LANES)
        a8, q = row - b, col - r
        cols = [pl.ds(pl.multiple_of(q + j * LANES, LANES), LANES) for j in range(3)]
        at = lambda off: pl.ds(pl.multiple_of(a8 + off, SUBS), chunk)
        at8 = pl.ds(pl.multiple_of(a8 + extent, SUBS), SUBS)
        return b, r, cols, at, at8

    def patch(where, p, i):
        b, r, cols, at, at8 = where
        c0 = jnp.where(lane >= r, ext[p, at(i), cols[0]], ext[p, at(i), cols[2]])
        c1 = ext[p, at(i), cols[1]]
        if i == 0:
            x0 = jnp.where(lane8 >= r, ext[p, at8, cols[0]], ext[p, at8, cols[2]])
            x1 = ext[p, at8, cols[1]]
            c0 = jnp.concatenate([jnp.where(sub8 >= b, c0[:SUBS], x0), c0[SUBS:]], axis=0)
            c1 = jnp.concatenate([jnp.where(sub8 >= b, c1[:SUBS], x1), c1[SUBS:]], axis=0)
        return c0, c1

    def left_mul(m, hi, lo):
        table = jnp.concatenate([mats[m, 0], mats[m, 1], mats[m, 0]], axis=1)
        return matmul(table, jnp.concatenate([hi, hi, lo], axis=0))

    def right_mul(hi, lo, m):
        table = jnp.concatenate([mats[m, 0], mats[m, 1], mats[m, 0]], axis=0)
        return matmul(jnp.concatenate([hi, hi, lo], axis=1), table)

    def front(s):
        where = place(s)
        b, r = where[:2]

        def turn(p, i):
            r0 = pltpu.roll(shifted[b, p, i:i + chunk, :LANES], r, 1)
            r1 = pltpu.roll(shifted[b, p, i:i + chunk, LANES:], r, 1)
            return jnp.where(lane >= r, r0, r1), jnp.where(lane >= r, r1, r0)

        def wave(i):
            o_re, o_im = patch(where, 0, i), patch(where, 1, i)
            p_re, p_im = turn(0, i), turn(1, i)
            out = []
            for j in range(2):
                js = slice(j * LANES, (j + 1) * LANES)
                turned[0, i:i + chunk, js] = p_re[j]
                turned[1, i:i + chunk, js] = p_im[j]
                out.append((p_re[j] * o_re[j] - p_im[j] * o_im[j], p_re[j] * o_im[j] + p_im[j] * o_re[j]))
            return out

        for i in range(0, half, chunk):
            top, bot = wave(i), wave(i + half)
            for j in range(2):
                js = slice(j * LANES, (j + 1) * LANES)
                for c in range(2):
                    for e, v in enumerate((top[j][c] + bot[j][c], top[j][c] - bot[j][c])):
                        hi, lo = parts(v)
                        sh_h[e, c * half + i:c * half + i + chunk, js] = hi
                        sh_l[e, c * half + i:c * half + i + chunk, js] = lo
            yield
        mids = []
        for e in range(2):
            y = left_mul(2 * e, sh_h[e], sh_l[e])
            mids.append((y[:half], y[half:]))
            yield
        far = []
        for e in range(2):
            rows = []
            for re, im in mids:
                if e == 0:
                    halves = [re[:, :half] + re[:, half:], im[:, :half] + im[:, half:]]
                else:
                    halves = [re[:, :half] - re[:, half:], im[:, :half] - im[:, half:]]
                rows.append(jnp.concatenate(halves, axis=1))
            hi, lo = parts(jnp.concatenate(rows, axis=0))
            far.append(right_mul(hi, lo, 2 * e + 1))
            yield
        m_rows = jnp.concatenate(
            [
                jnp.concatenate([meas[j, s, pl.ds(e, half, stride=2), :] for j in range(2)], axis=1)
                for e in range(2)
            ],
            axis=0,
        )
        m_hi, m_lo = parts(m_rows)
        amp = matmul(jnp.concatenate([m_hi, m_lo], axis=1), jnp.concatenate([pick[...]] * 2, axis=0))
        yield
        total = jnp.zeros((SUBS, LANES), F32)
        for e in range(2):
            re, im = far[e][:, :half], far[e][:, half:]
            t = re * re + im * im + 1.0
            inv = lax.rsqrt(t)
            differ = t * inv - amp[:, e * half:(e + 1) * half]
            total = total + jnp.sum((differ * differ).reshape(extent // SUBS, SUBS, half), axis=0)
            factor = differ * inv
            hi, lo = parts(jnp.concatenate([re * factor, im * factor], axis=1))
            z_h[e] = hi
            z_l[e] = lo
            yield
        loss_out[s] = total

    def back(s):
        where = place(s)
        b, r, cols, at, at8 = where
        backs = []
        for e in range(2):
            backs.append(right_mul(z_h[e], z_l[e], 2 * e))
            yield
        outs = []
        for e in range(2):
            rs = slice(e * half, (e + 1) * half)
            left, right = backs[0][rs] + backs[1][rs], backs[0][rs] - backs[1][rs]
            x = jnp.concatenate(
                [
                    jnp.concatenate([left[:, :half], right[:, :half]], axis=1),
                    jnp.concatenate([left[:, half:], right[:, half:]], axis=1),
                ],
                axis=0,
            )
            hi, lo = parts(x)
            outs.append(left_mul(2 * e + 1, hi, lo))
            yield
        for k in range(2):
            for i0 in range(0, half, chunk):
                i = k * half + i0
                o_re, o_im = patch(where, 0, i), patch(where, 1, i)
                q_re, q_im = [], []
                for j in range(2):
                    js = slice(j * LANES, (j + 1) * LANES)
                    pair = [(outs[0][at0:at0 + chunk, js], outs[1][at0:at0 + chunk, js]) for at0 in (i0, half + i0)]
                    b_re, b_im = [(u + v) if k == 0 else (u - v) for u, v in pair]
                    p_re, p_im = kept[0, i:i + chunk, js], kept[1, i:i + chunk, js]
                    g_re = p_re * b_re + p_im * b_im
                    g_im = p_re * b_im - p_im * b_re
                    q_re.append(o_re[j] * b_re + o_im[j] * b_im)
                    q_im.append(o_re[j] * b_im - o_im[j] * b_re)
                    for p, g in enumerate((g_re, g_im)):
                        if i == 0:
                            spill = jnp.where(sub8 < b, g[:SUBS], 0.0)
                            g = jnp.concatenate([jnp.where(sub8 >= b, g[:SUBS], 0.0), g[SUBS:]], axis=0)
                        if j == 0:
                            grad[p, at(i), cols[0]] += jnp.where(lane >= r, g, 0.0)
                            grad[p, at(i), cols[2]] += jnp.where(lane < r, g, 0.0)
                            if i == 0:
                                grad[p, at8, cols[0]] += jnp.where(lane8 >= r, spill, 0.0)
                                grad[p, at8, cols[2]] += jnp.where(lane8 < r, spill, 0.0)
                        else:
                            grad[p, at(i), cols[1]] += g
                            if i == 0:
                                grad[p, at8, cols[1]] += spill
                turn_back = lax.rem(LANES - r, LANES)
                for p, (h0, h1) in enumerate((q_re, q_im)):
                    h0 = pltpu.roll(h0, turn_back, 1)
                    h1 = pltpu.roll(h1, turn_back, 1)
                    keep = lane < LANES - r
                    accs[b, p, i:i + chunk, :LANES] += jnp.where(keep, h0, h1)
                    accs[b, p, i:i + chunk, LANES:] += jnp.where(keep, h1, h0)
                yield

    def run(streams, plan=""):
        left = dict(streams)
        for name in plan:
            next(left[name])
        for stream in left.values():
            for _ in stream:
                pass

    def keep_probe():
        for p in range(2):
            kept[p] = turned[p]

    def ready(s):
        for j in range(2):
            fetch(s, j).wait()

    @pl.when(count > 0)
    def _():
        ready(order[0])
        run({"f": front(order[0])})
        keep_probe()

    for c in late:
        c.wait()

    def step(t, c):
        ready(order[t])
        run({"b": back(order[t - 1]), "f": front(order[t])}, PLAN)
        keep_probe()
        return c

    lax.fori_loop(1, count, step, 0)

    @pl.when(count > 0)
    def _():
        run({"b": back(order[count - 1])})

    copies.clear()
    if inner:
        copy(grad.at[:, mid, mid], grad_out)
    else:
        for dst, (rows, cols) in zip(gsides, sides_out):
            copy(grad.at[:, rows, cols], dst)
        for box in ring:
            copy(own(grad, box, half), own(grad_out, box, 0))
    for p in range(2):
        acc = accs[0, p]
        for b in range(1, SUBS):
            acc = acc + pltpu.roll(accs[b, p], extent - b, 0)
        for j in range(extent // LANES):
            at = pl.ds((p * (extent // LANES) + j) * extent, extent)
            part = acc[:, j * LANES:(j + 1) * LANES]
            acc_out[at, :] = part if inner else part + acc_in[at, :]
    for c in copies:
        c.wait()


def run_slots(phase, centers, live, tile_obj, probe, measured, tables, extra=()):
    extent = probe.shape[1]
    half = extent // 2
    slots = centers.shape[0]
    tile = tile_obj.shape[1]
    size = tile + 2 * half
    inner = phase == "inner"
    smem = pl.BlockSpec(memory_space=pltpu.SMEM)
    hbm = pl.BlockSpec(memory_space=pl.ANY)
    vmem = pl.BlockSpec(memory_space=pltpu.VMEM)
    in_specs = [smem, smem, hbm, vmem, hbm, vmem, vmem]
    out_shape = [
        jax.ShapeDtypeStruct((2, tile, tile), F32),
        jax.ShapeDtypeStruct((2 * extent * extent // LANES, LANES), F32),
        jax.ShapeDtypeStruct((slots, SUBS, LANES), F32),
    ]
    out_specs = [hbm, vmem, vmem]
    if not inner:
        in_specs += [hbm] * 5 + [vmem, vmem]
        out_shape += [jax.ShapeDtypeStruct((2, half, tile), F32)] * 2
        out_shape += [jax.ShapeDtypeStruct((2, tile, half), F32)] * 2
        out_shape += [jax.ShapeDtypeStruct((2, half, half), F32)] * 4
        out_specs += [hbm] * 8
    flops = slots * 16 * 2 * extent**3
    return pl.pallas_call(
        functools.partial(slot_kernel, phase, extent, slots, tile),
        out_shape=out_shape,
        in_specs=in_specs,
        out_specs=out_specs,
        scratch_shapes=[
            pltpu.VMEM((2, size, size), F32),
            pltpu.VMEM((2, size, size), F32),
            pltpu.VMEM((SUBS, 2, extent, extent), F32),
            pltpu.VMEM((SUBS, 2, extent, extent), F32),
            pltpu.VMEM((2, extent, extent), F32),
            pltpu.VMEM((2, extent, extent), F32),
            pltpu.VMEM((2, slots, extent, LANES), F32),
            pltpu.VMEM((2, extent, extent), BF),
            pltpu.VMEM((2, extent, extent), BF),
            pltpu.VMEM((2, extent, extent), BF),
            pltpu.VMEM((2, extent, extent), BF),
            pltpu.SemaphoreType.DMA((16,)),
            pltpu.SemaphoreType.DMA((2, slots)),
            pltpu.SMEM((slots + 1,), jnp.int32),
        ],
        compiler_params=pltpu.CompilerParams(vmem_limit_bytes=60 * 2**20),
        cost_estimate=pl.CostEstimate(flops=flops, bytes_accessed=32 * 2**20, transcendentals=0),
        input_output_aliases={} if inner else {len(in_specs) - 3: 0},
    )(centers, live, tile_obj, probe, measured, *tables, *extra)


def send(y, axis, stride, count, k):
    n = lax.axis_size(axis)
    spot = lambda i: (i // stride) % count
    pairs = [(i, i + ((spot(i) + k) % count - spot(i)) * stride) for i in range(n)]
    return lax.ppermute(y, axis, pairs)


def sum_all(x, groups, scale, shape):
    flat = x
    axis, stride, last = groups[-1]
    whole = last & (last - 1) == 0
    split = groups[:-1] if whole else groups
    places = [lax.rem(lax.axis_index(axis) // stride, count) for axis, stride, count in split]
    for level, (axis, stride, count) in enumerate(split):
        me = places[level]
        rows = flat.shape[0] // count
        own = lax.dynamic_slice_in_dim(flat, me * rows, rows, 0)
        got = [
            send(lax.dynamic_slice_in_dim(flat, lax.rem(me + k, count) * rows, rows, 0), axis, stride, count, k)
            for k in range(1, count)
        ]
        flat = sum(got, own)
    if whole:
        axis, stride, count = groups[-1]
        n = lax.axis_size(axis)
        tree = [flat] + [lax.ppermute(flat, axis, [(i, i ^ (k * stride)) for i in range(n)]) for k in range(1, count)]
        while len(tree) > 1:
            tree = [tree[k] + tree[k + 1] for k in range(0, len(tree), 2)]
        flat = tree[0]
    for level, (axis, stride, count) in reversed(list(enumerate(split))):
        me = places[level]
        pieces = [flat] + [send(flat, axis, stride, count, k) for k in range(1, count)]
        if level == 0 and count == 2:
            return finish(me, pieces, scale, shape)
        rows = flat.shape[0]
        out = jnp.zeros((count * rows, LANES), F32)
        for k, piece in enumerate(pieces):
            out = lax.dynamic_update_slice_in_dim(out, piece, lax.rem(me + count - k, count) * rows, 0)
        flat = out
    return finish(jnp.int32(0), [flat], scale, shape)


def finish_kernel(scale, me, *refs):
    pieces, out = refs[:-1], refs[-1]
    planes, extent, width = out.shape
    each = planes // len(pieces)
    for k, piece in enumerate(pieces):
        owner = me[0] if k == 0 else len(pieces) - 1 - me[0]
        for p in range(each):
            for j in range(width // LANES):
                at = (p * (width // LANES) + j) * extent
                out[owner * each + p, :, j * LANES:(j + 1) * LANES] = piece[at:at + extent, :] * scale


def finish(me, pieces, scale, shape):
    vmem = pl.BlockSpec(memory_space=pltpu.VMEM)
    return pl.pallas_call(
        functools.partial(finish_kernel, scale),
        out_shape=jax.ShapeDtypeStruct(shape, F32),
        in_specs=[pl.BlockSpec(memory_space=pltpu.SMEM)] + [vmem] * len(pieces),
        out_specs=vmem,
        compiler_params=pltpu.CompilerParams(vmem_limit_bytes=8 * 2**20),
        cost_estimate=pl.CostEstimate(flops=2**17, bytes_accessed=2**20, transcendentals=0),
        name="finish",
    )(me.reshape(1), *pieces)


def sum_groups():
    nx, ny = lax.axis_size("gx"), lax.axis_size("gy")
    groups = [("gx", 1, 2), ("gx", 2, nx // 2)] if nx % 2 == 0 else [("gx", 1, nx)]
    return [g for g in groups + [("gy", 1, ny)] if g[2] > 1]


def fold_kernel(half, tile, main, *refs):
    adds = refs[:4]
    corners = refs[4:8]
    out, rows_buf, cols_buf, rows_add, cols_add, corner_add, sems = refs[8:]
    del main
    inside = tile - 2 * half
    copies = []

    def copy(src, dst):
        copies.append(pltpu.make_async_copy(src, dst, sems.at[len(copies)]))
        copies[-1].start()

    far = tile - half
    rows_at = [out.at[:, pl.ds(r, half), :] for r in (0, far)]
    cols_at = [out.at[:, pl.ds(half, inside), pl.ds(c, half)] for c in (0, far)]
    for k in range(2):
        copy(rows_at[k], rows_buf.at[k])
        copy(adds[k], rows_add.at[k])
        copy(cols_at[k], cols_buf.at[k])
        copy(adds[2 + k], cols_add.at[k])
    for k in range(4):
        copy(corners[k], corner_add.at[k])
    for c in copies:
        c.wait()
    copies.clear()
    step = 4 * SUBS
    for k in range(2):
        def rows_body(i, c, k=k):
            at = pl.ds(pl.multiple_of(i * step, step), step)
            side_at = pl.ds(pl.multiple_of(i * step + k * far, step), step)
            for p in range(2):
                rows_buf[k, p, at, :] += rows_add[k, p, at, :]
                for j, c0 in enumerate((0, far)):
                    lanes = slice(c0, c0 + half)
                    rows_buf[k, p, at, lanes] += cols_add[j, p, side_at, :] + corner_add[2 * k + j, p, at, :]
            return c

        lax.fori_loop(0, half // step, rows_body, 0)
        copy(rows_buf.at[k], rows_at[k])

        def cols_body(i, c, k=k):
            at = pl.ds(pl.multiple_of(i * step, step), step)
            side_at = pl.ds(pl.multiple_of(half + i * step, step), step)
            for p in range(2):
                cols_buf[k, p, at, :] += cols_add[k, p, side_at, :]
            return c

        lax.fori_loop(0, inside // step, cols_body, 0)
        copy(cols_buf.at[k], cols_at[k])
    for c in copies:
        c.wait()


def fold(main, adds, corners):
    tile = main.shape[1]
    half = adds[0].shape[1]
    hbm = pl.BlockSpec(memory_space=pl.ANY)
    return pl.pallas_call(
        functools.partial(fold_kernel, half, tile),
        out_shape=jax.ShapeDtypeStruct(main.shape, F32),
        in_specs=[hbm] * 9,
        out_specs=hbm,
        scratch_shapes=[
            pltpu.VMEM((2, 2, half, tile), F32),
            pltpu.VMEM((2, 2, tile - 2 * half, half), F32),
            pltpu.VMEM((2, 2, half, tile), F32),
            pltpu.VMEM((2, 2, tile, half), F32),
            pltpu.VMEM((4, 2, half, half), F32),
            pltpu.SemaphoreType.DMA((12,)),
        ],
        input_output_aliases={0: 0},
        compiler_params=pltpu.CompilerParams(vmem_limit_bytes=24 * 2**20),
        cost_estimate=pl.CostEstimate(flops=2**21, bytes_accessed=14 * 2**20, transcendentals=0),
        name="fold",
    )(main, *adds, *corners)


def shift2(x, dx, dy):
    nx, ny = lax.axis_size("gx"), lax.axis_size("gy")
    pairs = [
        (i * ny + j, (i + dx) * ny + j + dy)
        for i in range(nx)
        for j in range(ny)
        if 0 <= i + dx < nx and 0 <= j + dy < ny
    ]
    return lax.ppermute(x, ("gx", "gy"), pairs)


def on_device(object_field, probe, centers, live, measured):
    extent = probe.shape[1]
    half = extent // 2
    tile = object_field.shape[1]
    slots = centers.shape[0]
    tables = [jnp.asarray(t) for t in tables_np(extent)]
    far = tile - half
    ends = (slice(0, half), slice(far, tile))

    end_left = shift2(jnp.stack([object_field[:, e, far:] for e in ends]), 0, 1)
    end_right = shift2(jnp.stack([object_field[:, e, :half] for e in ends]), 0, -1)
    left = shift2(object_field[:, :, far:], 0, 1)
    right = shift2(object_field[:, :, :half], 0, -1)
    edges = [jnp.concatenate([end_left[k], object_field[:, ends[k]], end_right[k]], axis=2) for k in range(2)]
    up = shift2(edges[1], 1, 0)
    down = shift2(edges[0], -1, 0)
    grad_a, acc_a, loss_a = run_slots("inner", centers, live, object_field, probe, measured, tables)
    grad_b, acc_b, loss_b, gup, gdown, gleft, gright, *gcorners = run_slots(
        "outer", centers, live, object_field, probe, measured, tables,
        (up, down, left, right, grad_a, acc_a, loss_a),
    )
    from_left = shift2(gright, 0, 1)
    from_right = shift2(gleft, 0, -1)
    from_up = shift2(gdown, 1, 0)
    from_down = shift2(gup, -1, 0)
    steps = ((-1, -1), (-1, 1), (1, -1), (1, 1))
    corners = [shift2(g, dx, dy) for g, (dx, dy) in zip(gcorners, steps)][::-1]
    slots_all = slots * lax.axis_size("gx") * lax.axis_size("gy")
    probe_grad = sum_all(acc_b, sum_groups(), 1.0 / math.sqrt(slots_all), probe.shape)
    object_grad = fold(grad_b, (from_up, from_down, from_left, from_right), corners)

    slot_loss = jnp.sum(loss_b, axis=(1, 2)) * (0.5 / (extent * extent))
    return object_grad, probe_grad, slot_loss


def solution(mesh):
    placed = (
        P(None, "gx", "gy"),
        P(),
        P(("gx", "gy"), None),
        P(("gx", "gy")),
        P(("gx", "gy"), None, None),
    )
    return jax.shard_map(
        on_device,
        mesh=mesh,
        in_specs=placed,
        out_specs=(P(None, "gx", "gy"), P(), P(("gx", "gy"))),
        check_vma=False,
    )
```

```python
import functools
import math

import jax
import jax.numpy as jnp
import numpy as np
from jax import lax
from jax.experimental import pallas as pl
from jax.experimental.pallas import tpu as pltpu
from jax.sharding import PartitionSpec as P


LANES = 128
SUBS = 8
AHEAD = 1
PLAN = "bfbfbfbfbfbfbfbfbfbfbfb"
BF = jnp.bfloat16
F32 = jnp.float32


def split_np(table):
    hi = table.astype(np.float32).astype(jnp.bfloat16)
    lo = (table - hi.astype(np.float64)).astype(np.float32).astype(jnp.bfloat16)
    return hi, lo


def tables_np(extent):
    half = extent // 2
    k = np.arange(extent)[:, None]
    n = np.arange(half)[None, :]
    angle = -2.0 * np.pi * ((k * n) % extent) / extent
    re = np.cos(angle) / math.sqrt(extent)
    im = np.sin(angle) / math.sqrt(extent)
    mats = []
    for parity in range(2):
        a, b = re[parity::2], im[parity::2]
        left = np.block([[a, -b], [b, a]])
        mats += [np.stack(split_np(left)), np.stack(split_np(left.T))]
    pick = np.zeros((extent, extent), np.float32)
    pick[2 * np.arange(half), np.arange(half)] = 1
    pick[2 * np.arange(half) + 1, half + np.arange(half)] = 1
    return np.stack(mats), pick.astype(jnp.bfloat16)


def parts(x):
    hi = x.astype(BF)
    lo = (x - hi.astype(F32)).astype(BF)
    return hi, lo


def matmul(a, b):
    return jnp.dot(a, b, preferred_element_type=F32)


def slot_kernel(
    phase, extent, slots, tile,
    centers, live, side, *refs,
):
    half = extent // 2
    inner = phase == "inner"
    it = iter(refs)
    take = lambda n: [next(it) for _ in range(n)]
    tile_hbm, probe, meas_hbm, mats, pick = take(5)
    if not inner:
        sides_hbm = take(4)
        grad_in, keep_in, send_in, loss_in = take(4)
        del grad_in
    grad_out, keep_out, send_out, loss_out = take(4)
    if not inner:
        gsides = take(8)
    ext, grad, shifted, accs, turned, kept, meas, sh_h, sh_l, z_h, z_l, in_sems, out_sems, msems, order, keys = take(16)
    mid = pl.ds(half, tile)
    low, high = pl.ds(0, half), pl.ds(half + tile, half)
    whole = pl.ds(0, 2 * half + tile)
    bands = tile // half
    first, limit = (1, bands + 1) if inner else (0, bands + 2)

    def band_copies(k, pairs, sems):
        return [pltpu.make_async_copy(src, dst, sems.at[i, k]) for i, (src, dst) in enumerate(pairs)]

    def band_loads(k, edge=None):
        if edge is not None:
            rows = (low, high)[edge]
            return band_copies(k, [(sides_hbm[edge], ext.at[:, rows, whole])], in_sems)
        there = pl.ds(pl.multiple_of(k * half, half), half)
        here = pl.ds(pl.multiple_of((k - 1) * half, half), half)
        pairs = [(tile_hbm.at[:, here, :], ext.at[:, there, mid])]
        if not inner:
            pairs.append((sides_hbm[2].at[:, here, :], ext.at[:, there, low]))
            pairs.append((sides_hbm[3].at[:, here, :], ext.at[:, there, high]))
            pairs.append((grad_out.at[:, here, :], grad.at[:, there, mid]))
        return band_copies(k, pairs, in_sems)

    def band_stores(k, edge=None):
        if edge is not None:
            rows = (low, high)[edge]
            pairs = [(grad.at[:, rows, mid], gsides[edge])]
            pairs += [(grad.at[:, rows, cols], gsides[4 + 2 * edge + j]) for j, cols in enumerate((low, high))]
            return band_copies(k, pairs, out_sems)
        there = pl.ds(pl.multiple_of(k * half, half), half)
        here = pl.ds(pl.multiple_of((k - 1) * half, half), half)
        pairs = [(grad.at[:, there, mid], grad_out.at[:, here, :])]
        if not inner:
            pairs.append((grad.at[:, there, low], gsides[2].at[:, here, :]))
            pairs.append((grad.at[:, there, high], gsides[3].at[:, here, :]))
        return band_copies(k, pairs, out_sems)

    def on_bands(start, stop, copies_of, act):
        def body(k, c):
            if inner:
                act(copies_of(k))
                return c
            for edge, at in enumerate((0, bands + 1)):
                @pl.when(k == at)
                def _(edge=edge, at=at):
                    act(copies_of(at, edge))

            @pl.when((k > 0) & (k <= bands))
            def _():
                act(copies_of(k))

            return c

        stop = jnp.maximum(start, stop)
        lax.fori_loop(start, stop, body, 0)
        return stop

    def start_all(copies):
        for c in copies:
            c.start()

    def wait_all(copies):
        for c in copies:
            c.wait()

    def wanted(s):
        row = centers[s, 0]
        col = centers[s, 1]
        inside = (row >= half) & (row <= tile - half) & (col >= half) & (col <= tile - half)
        return (live[s] > 0) & (inside if inner else jnp.logical_not(inside))

    def fetch(s, j):
        return pltpu.make_async_copy(meas_hbm.at[s, :, pl.ds(j * LANES, LANES)], meas.at[j, s], msems.at[j, s])

    issued = on_bands(jnp.int32(first), jnp.int32(min(first + 3, limit)), band_loads, start_all)

    far_key = (2 * half + tile) * slots

    def set_key(s, n):
        go = wanted(s)
        keys[s] = jnp.where(go, centers[s, 0] * slots, far_key) + s
        return n + go.astype(jnp.int32)

    count = lax.fori_loop(0, slots, set_key, jnp.int32(0))

    def set_order(s, c):
        own = keys[s]
        rank = jnp.int32(0)
        for u in range(slots):
            rank = rank + (keys[u] < own).astype(jnp.int32)
        order[rank] = s
        return c

    lax.fori_loop(0, slots, set_order, 0)

    def frame_row(s):
        row = centers[s, 0]
        return row - lax.rem(row, SUBS)

    def reach(s, more=0):
        return jnp.minimum((frame_row(s) + extent + SUBS - 1) // half + 1 + more, limit)

    def ask(issued, s):
        return on_bands(issued, reach(s, AHEAD), band_loads, start_all)

    def arrive(waited, s):
        return on_bands(waited, reach(s), band_loads, wait_all)

    issued = ask(issued, order[0])

    def prefetch(t, c):
        for j in range(2):
            fetch(order[t], j).start()
        return c

    lax.fori_loop(0, count, prefetch, 0)

    for p in range(2):
        plane = probe[p]
        for b in range(SUBS):
            shifted[b, p] = pltpu.roll(plane, b, 0) if b else plane
    accs[...] = jnp.zeros_like(accs)
    step_rows = 4 * SUBS

    def clear(rows, cols):
        block = jnp.zeros((2, step_rows, cols.size), F32)

        def body(i, c):
            at = pl.multiple_of(rows.start + i * step_rows, step_rows)
            grad[:, pl.ds(at, step_rows), cols] = block
            return c

        lax.fori_loop(0, rows.size // step_rows, body, 0)

    if inner:
        loss_out[...] = jnp.zeros_like(loss_out)
        clear(mid, mid)
    else:
        loss_out[...] = loss_in[...]
        for rows, cols in ((low, whole), (high, whole), (mid, low), (mid, high)):
            clear(rows, cols)

    chunk = 32
    lane8 = lax.broadcasted_iota(jnp.int32, (SUBS, LANES), 1)
    sub8 = lax.broadcasted_iota(jnp.int32, (SUBS, LANES), 0)

    lane = lax.broadcasted_iota(jnp.int32, (chunk, LANES), 1)

    def place(s):
        row, col = centers[s, 0], centers[s, 1]
        b, r = lax.rem(row, SUBS), lax.rem(col, LANES)
        a8, q = row - b, col - r
        cols = [pl.ds(pl.multiple_of(q + j * LANES, LANES), LANES) for j in range(3)]
        at = lambda off: pl.ds(pl.multiple_of(a8 + off, SUBS), chunk)
        at8 = pl.ds(pl.multiple_of(a8 + extent, SUBS), SUBS)
        return b, r, cols, at, at8

    def patch(where, p, i):
        b, r, cols, at, at8 = where
        c0 = jnp.where(lane >= r, ext[p, at(i), cols[0]], ext[p, at(i), cols[2]])
        c1 = ext[p, at(i), cols[1]]
        if i == 0:
            x0 = jnp.where(lane8 >= r, ext[p, at8, cols[0]], ext[p, at8, cols[2]])
            x1 = ext[p, at8, cols[1]]
            c0 = jnp.concatenate([jnp.where(sub8 >= b, c0[:SUBS], x0), c0[SUBS:]], axis=0)
            c1 = jnp.concatenate([jnp.where(sub8 >= b, c1[:SUBS], x1), c1[SUBS:]], axis=0)
        return c0, c1

    def left_mul(m, hi, lo):
        table = jnp.concatenate([mats[m, 0], mats[m, 1], mats[m, 0]], axis=1)
        return matmul(table, jnp.concatenate([hi, hi, lo], axis=0))

    def right_mul(hi, lo, m):
        table = jnp.concatenate([mats[m, 0], mats[m, 1], mats[m, 0]], axis=0)
        return matmul(jnp.concatenate([hi, hi, lo], axis=1), table)

    def front(s):
        where = place(s)
        b, r = where[:2]

        def turn(p, i):
            r0 = pltpu.roll(shifted[b, p, i:i + chunk, :LANES], r, 1)
            r1 = pltpu.roll(shifted[b, p, i:i + chunk, LANES:], r, 1)
            return jnp.where(lane >= r, r0, r1), jnp.where(lane >= r, r1, r0)

        def wave(i):
            o_re, o_im = patch(where, 0, i), patch(where, 1, i)
            p_re, p_im = turn(0, i), turn(1, i)
            out = []
            for j in range(2):
                js = slice(j * LANES, (j + 1) * LANES)
                turned[0, i:i + chunk, js] = p_re[j]
                turned[1, i:i + chunk, js] = p_im[j]
                out.append((p_re[j] * o_re[j] - p_im[j] * o_im[j], p_re[j] * o_im[j] + p_im[j] * o_re[j]))
            return out

        for i in range(0, half, chunk):
            top, bot = wave(i), wave(i + half)
            for j in range(2):
                js = slice(j * LANES, (j + 1) * LANES)
                for c in range(2):
                    for e, v in enumerate((top[j][c] + bot[j][c], top[j][c] - bot[j][c])):
                        hi, lo = parts(v)
                        sh_h[e, c * half + i:c * half + i + chunk, js] = hi
                        sh_l[e, c * half + i:c * half + i + chunk, js] = lo
            yield
        mids = []
        for e in range(2):
            y = left_mul(2 * e, sh_h[e], sh_l[e])
            mids.append((y[:half], y[half:]))
            yield
        far = []
        for e in range(2):
            rows = []
            for re, im in mids:
                if e == 0:
                    halves = [re[:, :half] + re[:, half:], im[:, :half] + im[:, half:]]
                else:
                    halves = [re[:, :half] - re[:, half:], im[:, :half] - im[:, half:]]
                rows.append(jnp.concatenate(halves, axis=1))
            hi, lo = parts(jnp.concatenate(rows, axis=0))
            far.append(right_mul(hi, lo, 2 * e + 1))
            yield
        m_rows = jnp.concatenate(
            [
                jnp.concatenate([meas[j, s, pl.ds(e, half, stride=2), :] for j in range(2)], axis=1)
                for e in range(2)
            ],
            axis=0,
        )
        m_hi, m_lo = parts(m_rows)
        amp = matmul(jnp.concatenate([m_hi, m_lo], axis=1), jnp.concatenate([pick[...]] * 2, axis=0))
        yield
        total = jnp.zeros((SUBS, LANES), F32)
        for e in range(2):
            re, im = far[e][:, :half], far[e][:, half:]
            t = re * re + im * im + 1.0
            inv = lax.rsqrt(t)
            differ = t * inv - amp[:, e * half:(e + 1) * half]
            total = total + jnp.sum((differ * differ).reshape(extent // SUBS, SUBS, half), axis=0)
            factor = differ * inv
            hi, lo = parts(jnp.concatenate([re * factor, im * factor], axis=1))
            z_h[e] = hi
            z_l[e] = lo
            yield
        loss_out[s] = total * (0.5 / (extent * extent))

    def back(s):
        where = place(s)
        b, r, cols, at, at8 = where
        backs = []
        for e in range(2):
            backs.append(right_mul(z_h[e], z_l[e], 2 * e))
            yield
        outs = []
        for e in range(2):
            rs = slice(e * half, (e + 1) * half)
            left, right = backs[0][rs] + backs[1][rs], backs[0][rs] - backs[1][rs]
            x = jnp.concatenate(
                [
                    jnp.concatenate([left[:, :half], right[:, :half]], axis=1),
                    jnp.concatenate([left[:, half:], right[:, half:]], axis=1),
                ],
                axis=0,
            )
            hi, lo = parts(x)
            outs.append(left_mul(2 * e + 1, hi, lo))
            yield
        for k in range(2):
            for i0 in range(0, half, chunk):
                i = k * half + i0
                o_re, o_im = patch(where, 0, i), patch(where, 1, i)
                q_re, q_im = [], []
                for j in range(2):
                    js = slice(j * LANES, (j + 1) * LANES)
                    pair = [(outs[0][at0:at0 + chunk, js], outs[1][at0:at0 + chunk, js]) for at0 in (i0, half + i0)]
                    b_re, b_im = [(u + v) if k == 0 else (u - v) for u, v in pair]
                    p_re, p_im = kept[0, i:i + chunk, js], kept[1, i:i + chunk, js]
                    g_re = p_re * b_re + p_im * b_im
                    g_im = p_re * b_im - p_im * b_re
                    q_re.append(o_re[j] * b_re + o_im[j] * b_im)
                    q_im.append(o_re[j] * b_im - o_im[j] * b_re)
                    for p, g in enumerate((g_re, g_im)):
                        if i == 0:
                            spill = jnp.where(sub8 < b, g[:SUBS], 0.0)
                            g = jnp.concatenate([jnp.where(sub8 >= b, g[:SUBS], 0.0), g[SUBS:]], axis=0)
                        if j == 0:
                            grad[p, at(i), cols[0]] += jnp.where(lane >= r, g, 0.0)
                            grad[p, at(i), cols[2]] += jnp.where(lane < r, g, 0.0)
                            if i == 0:
                                grad[p, at8, cols[0]] += jnp.where(lane8 >= r, spill, 0.0)
                                grad[p, at8, cols[2]] += jnp.where(lane8 < r, spill, 0.0)
                        else:
                            grad[p, at(i), cols[1]] += g
                            if i == 0:
                                grad[p, at8, cols[1]] += spill
                turn_back = lax.rem(LANES - r, LANES)
                for p, (h0, h1) in enumerate((q_re, q_im)):
                    h0 = pltpu.roll(h0, turn_back, 1)
                    h1 = pltpu.roll(h1, turn_back, 1)
                    keep = lane < LANES - r
                    accs[b, p, i:i + chunk, :LANES] += jnp.where(keep, h0, h1)
                    accs[b, p, i:i + chunk, LANES:] += jnp.where(keep, h1, h0)
                yield

    def run(streams, plan=""):
        left = dict(streams)
        for name in plan:
            next(left[name])
        for stream in left.values():
            for _ in stream:
                pass

    def keep_probe():
        for p in range(2):
            kept[p] = turned[p]

    def ready(s):
        for j in range(2):
            fetch(s, j).wait()

    def leave(stored, s):
        return on_bands(stored, frame_row(s) // half, band_stores, start_all)

    waited = arrive(jnp.int32(first), order[0])
    issued = ask(issued, order[jnp.minimum(1, slots - 1)])

    @pl.when(count > 0)
    def _():
        ready(order[0])
        run({"f": front(order[0])})
        keep_probe()

    def step(t, c):
        issued, waited, stored = c
        ready(order[t])
        waited = arrive(waited, order[t])
        issued = ask(issued, order[jnp.minimum(t + 1, slots - 1)])
        stored = leave(stored, order[t - 1])
        run({"b": back(order[t - 1]), "f": front(order[t])}, PLAN)
        keep_probe()
        return issued, waited, stored

    issued, waited, stored = lax.fori_loop(1, count, step, (issued, waited, jnp.int32(first)))
    on_bands(issued, jnp.int32(limit), band_loads, start_all)
    on_bands(waited, jnp.int32(limit), band_loads, wait_all)
    last = order[jnp.maximum(count, 1) - 1]
    stored = leave(stored, last)

    @pl.when(count > 0)
    def _():
        run({"b": back(last)})

    on_bands(stored, jnp.int32(limit), band_stores, start_all)
    for k, dst in enumerate((keep_out, send_out)):
        p = side[0] if k == 0 else 1 - side[0]
        acc = accs[0, p]
        for b in range(1, SUBS):
            acc = acc + pltpu.roll(accs[b, p], extent - b, 0)
        for j in range(extent // LANES):
            at = pl.ds(j * extent, extent)
            part = acc[:, j * LANES:(j + 1) * LANES]
            dst[at, :] = part if inner else part + (keep_in, send_in)[k][at, :]
    on_bands(jnp.int32(first), jnp.int32(limit), band_stores, wait_all)


def run_slots(phase, centers, live, side, tile_obj, probe, measured, tables, extra=()):
    extent = probe.shape[1]
    half = extent // 2
    slots = centers.shape[0]
    tile = tile_obj.shape[1]
    size = tile + 2 * half
    inner = phase == "inner"
    smem = pl.BlockSpec(memory_space=pltpu.SMEM)
    hbm = pl.BlockSpec(memory_space=pl.ANY)
    vmem = pl.BlockSpec(memory_space=pltpu.VMEM)
    in_specs = [smem, smem, smem, hbm, vmem, hbm, vmem, vmem]
    out_shape = [
        jax.ShapeDtypeStruct((2, tile, tile), F32),
        jax.ShapeDtypeStruct((extent * extent // LANES, LANES), F32),
        jax.ShapeDtypeStruct((extent * extent // LANES, LANES), F32),
        jax.ShapeDtypeStruct((slots, SUBS, LANES), F32),
    ]
    out_specs = [hbm, vmem, vmem, vmem]
    if not inner:
        in_specs += [hbm] * 5 + [vmem, vmem, vmem]
        out_shape += [jax.ShapeDtypeStruct((2, half, tile), F32)] * 2
        out_shape += [jax.ShapeDtypeStruct((2, tile, half), F32)] * 2
        out_shape += [jax.ShapeDtypeStruct((2, half, half), F32)] * 4
        out_specs += [hbm] * 8
    flops = slots * 16 * 2 * extent**3
    return pl.pallas_call(
        functools.partial(slot_kernel, phase, extent, slots, tile),
        out_shape=out_shape,
        in_specs=in_specs,
        out_specs=out_specs,
        scratch_shapes=[
            pltpu.VMEM((2, size, size), F32),
            pltpu.VMEM((2, size, size), F32),
            pltpu.VMEM((SUBS, 2, extent, extent), F32),
            pltpu.VMEM((SUBS, 2, extent, extent), F32),
            pltpu.VMEM((2, extent, extent), F32),
            pltpu.VMEM((2, extent, extent), F32),
            pltpu.VMEM((2, slots, extent, LANES), F32),
            pltpu.VMEM((2, extent, extent), BF),
            pltpu.VMEM((2, extent, extent), BF),
            pltpu.VMEM((2, extent, extent), BF),
            pltpu.VMEM((2, extent, extent), BF),
            pltpu.SemaphoreType.DMA((4, tile // half + 2)),
            pltpu.SemaphoreType.DMA((3, tile // half + 2)),
            pltpu.SemaphoreType.DMA((2, slots)),
            pltpu.SMEM((slots,), jnp.int32),
            pltpu.SMEM((slots,), jnp.int32),
        ],
        compiler_params=pltpu.CompilerParams(vmem_limit_bytes=60 * 2**20),
        cost_estimate=pl.CostEstimate(flops=flops, bytes_accessed=32 * 2**20, transcendentals=0),
        input_output_aliases={} if inner else {len(in_specs) - 4: 0},
    )(centers, live, side, tile_obj, probe, measured, *tables, *extra)


def send(y, axis, stride, count, k):
    n = lax.axis_size(axis)
    spot = lambda i: (i // stride) % count
    pairs = [(i, i + ((spot(i) + k) % count - spot(i)) * stride) for i in range(n)]
    return lax.ppermute(y, axis, pairs)


def sum_all(keep, other, groups, scale, shape):
    (axis, stride, count), (last_axis, last_stride, last) = groups
    me = lax.rem(lax.axis_index(axis) // stride, count)
    got = send(other, axis, 1, 2, 1)
    flat = keep + got
    rows = flat.shape[0] // count
    own = lax.dynamic_slice_in_dim(flat, me * rows, rows, 0)
    got = [
        send(lax.dynamic_slice_in_dim(flat, lax.rem(me + k, count) * rows, rows, 0), axis, stride, count, k)
        for k in range(1, count)
    ]
    flat = sum(got, own)
    n = lax.axis_size(last_axis)
    tree = [flat] + [
        lax.ppermute(flat, last_axis, [(i, i ^ (k * last_stride)) for i in range(n)]) for k in range(1, last)
    ]
    while len(tree) > 1:
        tree = [tree[k] + tree[k + 1] for k in range(0, len(tree), 2)]
    flat = tree[0]
    pieces = [flat] + [send(flat, axis, stride, count, k) for k in range(1, count)]
    mine = jnp.concatenate(pieces, axis=0)
    theirs = send(mine, axis, 1, 2, 1)
    place = jnp.stack([lax.rem(lax.axis_index(axis), 2), me]).astype(jnp.int32)
    return finish(place, (mine, theirs), count, scale, shape)


def finish_kernel(scale, count, place, *refs):
    out = refs[-1]
    extent = out.shape[1]
    rows = refs[0].shape[0] // count
    for h, half_sum in enumerate(refs[:-1]):
        p = place[0] if h == 0 else 1 - place[0]
        for k in range(count):
            at = lax.rem(place[1] + count - k, count) * rows
            j = at // extent
            there = pl.ds(pl.multiple_of(at - j * extent, SUBS), rows)
            lanes = pl.ds(pl.multiple_of(j * LANES, LANES), LANES)
            out[p, there, lanes] = half_sum[k * rows:(k + 1) * rows, :] * scale


def finish(place, halves, count, scale, shape):
    vmem = pl.BlockSpec(memory_space=pltpu.VMEM)
    return pl.pallas_call(
        functools.partial(finish_kernel, scale, count),
        out_shape=jax.ShapeDtypeStruct(shape, F32),
        in_specs=[pl.BlockSpec(memory_space=pltpu.SMEM)] + [vmem] * 2,
        out_specs=vmem,
        compiler_params=pltpu.CompilerParams(vmem_limit_bytes=8 * 2**20),
        cost_estimate=pl.CostEstimate(flops=2**17, bytes_accessed=2**20, transcendentals=0),
        name="finish",
    )(place, *halves)


def sum_plain(keep, other, side, scale, shape):
    planes = jnp.where(side[0] == 0, jnp.stack([keep, other]), jnp.stack([other, keep]))
    totals = lax.psum(planes, ("gx", "gy")).reshape(2, -1, shape[1], LANES)
    return totals.transpose(0, 2, 1, 3).reshape(shape) * scale


def sum_groups(extent):
    nx, ny = lax.axis_size("gx"), lax.axis_size("gy")
    count = nx // 2
    fits = nx % 2 == 0 and ny & (ny - 1) == 0 and ny > 1 and count > 1
    fits = fits and (extent * extent // LANES) % (count * SUBS) == 0 and extent % (extent * extent // LANES // count) == 0
    return [("gx", 2, count), ("gy", 1, ny)] if fits else None


def fold_kernel(half, tile, main, *refs):
    adds = refs[:4]
    corners = refs[4:8]
    out, rows_buf, cols_buf, rows_add, cols_add, corner_add, sems = refs[8:]
    del main
    inside = tile - 2 * half
    copies = []

    def copy(src, dst):
        copies.append(pltpu.make_async_copy(src, dst, sems.at[len(copies)]))
        copies[-1].start()

    far = tile - half
    rows_at = [out.at[:, pl.ds(r, half), :] for r in (0, far)]
    cols_at = [out.at[:, pl.ds(half, inside), pl.ds(c, half)] for c in (0, far)]
    for k in range(2):
        copy(rows_at[k], rows_buf.at[k])
        copy(adds[k], rows_add.at[k])
        copy(cols_at[k], cols_buf.at[k])
        copy(adds[2 + k], cols_add.at[k])
    for k in range(4):
        copy(corners[k], corner_add.at[k])
    for c in copies:
        c.wait()
    copies.clear()
    step = 4 * SUBS
    for k in range(2):
        def rows_body(i, c, k=k):
            at = pl.ds(pl.multiple_of(i * step, step), step)
            side_at = pl.ds(pl.multiple_of(i * step + k * far, step), step)
            for p in range(2):
                rows_buf[k, p, at, :] += rows_add[k, p, at, :]
                for j, c0 in enumerate((0, far)):
                    lanes = slice(c0, c0 + half)
                    rows_buf[k, p, at, lanes] += cols_add[j, p, side_at, :] + corner_add[2 * k + j, p, at, :]
            return c

        lax.fori_loop(0, half // step, rows_body, 0)
        copy(rows_buf.at[k], rows_at[k])

        def cols_body(i, c, k=k):
            at = pl.ds(pl.multiple_of(i * step, step), step)
            side_at = pl.ds(pl.multiple_of(half + i * step, step), step)
            for p in range(2):
                cols_buf[k, p, at, :] += cols_add[k, p, side_at, :]
            return c

        lax.fori_loop(0, inside // step, cols_body, 0)
        copy(cols_buf.at[k], cols_at[k])
    for c in copies:
        c.wait()


def fold(main, adds, corners):
    tile = main.shape[1]
    half = adds[0].shape[1]
    hbm = pl.BlockSpec(memory_space=pl.ANY)
    return pl.pallas_call(
        functools.partial(fold_kernel, half, tile),
        out_shape=jax.ShapeDtypeStruct(main.shape, F32),
        in_specs=[hbm] * 9,
        out_specs=hbm,
        scratch_shapes=[
            pltpu.VMEM((2, 2, half, tile), F32),
            pltpu.VMEM((2, 2, tile - 2 * half, half), F32),
            pltpu.VMEM((2, 2, half, tile), F32),
            pltpu.VMEM((2, 2, tile, half), F32),
            pltpu.VMEM((4, 2, half, half), F32),
            pltpu.SemaphoreType.DMA((12,)),
        ],
        input_output_aliases={0: 0},
        compiler_params=pltpu.CompilerParams(vmem_limit_bytes=24 * 2**20),
        cost_estimate=pl.CostEstimate(flops=2**21, bytes_accessed=14 * 2**20, transcendentals=0),
        name="fold",
    )(main, *adds, *corners)


def shift2(x, dx, dy):
    nx, ny = lax.axis_size("gx"), lax.axis_size("gy")
    pairs = [
        (i * ny + j, (i + dx) * ny + j + dy)
        for i in range(nx)
        for j in range(ny)
        if 0 <= i + dx < nx and 0 <= j + dy < ny
    ]
    return lax.ppermute(x, ("gx", "gy"), pairs)


def on_device(object_field, probe, centers, live, measured):
    extent = probe.shape[1]
    half = extent // 2
    tile = object_field.shape[1]
    slots = centers.shape[0]
    tables = [jnp.asarray(t) for t in tables_np(extent)]
    far = tile - half
    ends = (slice(0, half), slice(far, tile))

    end_left = shift2(jnp.stack([object_field[:, e, far:] for e in ends]), 0, 1)
    end_right = shift2(jnp.stack([object_field[:, e, :half] for e in ends]), 0, -1)
    left = shift2(object_field[:, :, far:], 0, 1)
    right = shift2(object_field[:, :, :half], 0, -1)
    edges = [jnp.concatenate([end_left[k], object_field[:, ends[k]], end_right[k]], axis=2) for k in range(2)]
    up = shift2(edges[1], 1, 0)
    down = shift2(edges[0], -1, 0)
    groups = sum_groups(extent)
    side = lax.rem(lax.axis_index("gx"), 2).reshape(1)
    grad_a, keep_a, send_a, loss_a = run_slots("inner", centers, live, side, object_field, probe, measured, tables)
    grad_b, keep_b, send_b, loss_b, gup, gdown, gleft, gright, *gcorners = run_slots(
        "outer", centers, live, side, object_field, probe, measured, tables,
        (up, down, left, right, grad_a, keep_a, send_a, loss_a),
    )
    from_left = shift2(gright, 0, 1)
    from_right = shift2(gleft, 0, -1)
    from_up = shift2(gdown, 1, 0)
    from_down = shift2(gup, -1, 0)
    steps = ((-1, -1), (-1, 1), (1, -1), (1, 1))
    corners = [shift2(g, dx, dy) for g, (dx, dy) in zip(gcorners, steps)][::-1]
    slots_all = slots * lax.axis_size("gx") * lax.axis_size("gy")
    scale = 1.0 / math.sqrt(slots_all)
    if groups:
        probe_grad = sum_all(keep_b, send_b, groups, scale, probe.shape)
    else:
        probe_grad = sum_plain(keep_b, send_b, side, scale, probe.shape)
    object_grad = fold(grad_b, (from_up, from_down, from_left, from_right), corners)

    slot_loss = jnp.sum(loss_b, axis=(1, 2))
    return object_grad, probe_grad, slot_loss


def solution(mesh):
    placed = (
        P(None, "gx", "gy"),
        P(),
        P(("gx", "gy"), None),
        P(("gx", "gy")),
        P(("gx", "gy"), None, None),
    )
    return jax.shard_map(
        on_device,
        mesh=mesh,
        in_specs=placed,
        out_specs=(P(None, "gx", "gy"), P(), P(("gx", "gy"))),
        check_vma=False,
    )
```
